256 devices in a mesh: grp: 4 (over y), own: 64 (over x, z, core).
Axes of the slice: x: 4, y: 4, z: 8, core: 2. Of those that a mesh axis runs over, the one named last changes fastest.
Arguments:
- arrivals: bfloat16 [131072, 512], P(('grp', 'own')), may hold values from -6 to 6
- home_owner: int32 [131072, 1], P(('grp', 'own')), may hold values from 0 to 63; in each aligned block of 512 rows (0 to 511, 512 to 1023, ...) at most 16 rows name the same one
- cluster_slot: int32 [131072], P(('grp', 'own')), may hold values from 0 to 255
- bank: bfloat16 [16384, 32, 512], P('own'), may hold values from -6 to 6
- members: int32 [16384], P('own'), may hold values from 1 to 32
- centroid_sum: float32 [16384, 512], P('own'), may hold values from -1.6 to 1.6
Outputs:
- best_cosine: float32 [131072], P(('grp', 'own'))
- centroids: float32 [16384, 512], P('own')
The draws below stay inside these ranges and needn't reach their ends.
Inputs may be any that keep to these rules, and one draw needn't show every extreme that they name: `home_owner`: among the 512 rows of one device no value appears more than 16 times, and some value appears exactly 16 times.
All inputs are finite; a program needn't handle non-finite values.
Results may differ from the reference program's by a relative error of at most 0.0017.
Values may be sent and summed in bfloat16 or wider, within the bound.
A program may use at most 64 MiB of HBM per device.

```python
import math
import jax
import jax.numpy as jnp
import numpy as np
from jax import lax

D = 512
CL_DEV = 256
BLK = 32
TOK_DEV = 512
CLUSTERS = 16384
CAP = 16
ROWS = 131072
N_OWN = 64


def place_ends(drawn, stream_key, smallest, largest):
    longest = drawn.shape.index(max(drawn.shape))
    spots = []
    for shift in (0, 1):
        where = [jax.random.randint(jax.random.fold_in(stream_key, axis), (), 0, length) for axis, length in enumerate(drawn.shape)]
        where[longest] = (where[longest] + shift) % drawn.shape[longest]
        spots.append(tuple(where))
    return drawn.at[spots[0]].set(smallest).at[spots[1]].set(largest)


def levels(own_key, shape, shards, least, high):
    level = 1.0
    for position, blocks in shards:
        heights = jax.random.uniform(jax.random.fold_in(jax.random.fold_in(own_key, 6), position), (blocks,), jnp.float32, least / len(shards), high / len(shards))
        level = level * jnp.repeat(jnp.exp(heights), shape[position] // blocks).reshape((-1,) + (1,) * (len(shape) - 1 - position))
    return level


def shared_out(rng, own, number, rows, amount, top, most, lean):
    sequence = jax.random.permutation(rng, amount)
    heavy_load, usual = portions_of(amount, rows * top, most, lean, True), portions_of(amount, rows * top, most, lean, False)
    places = jnp.arange(amount)

    def named(tallies, rotation):
        used = int((tallies > 0).sum())
        fixed = max(1, used // 4)
        passed = fixed + (places - fixed + rotation * (used - fixed)) % max(1, amount - fixed)
        return jnp.zeros((amount,), jnp.int32).at[sequence[jnp.where(places < fixed, places, passed)]].set(jnp.asarray(tallies, jnp.int32))

    tallies = jnp.where(number % 4 == 0, named(heavy_load, number // 4), named(usual, number - number // 4 - 1))
    mixed = jax.random.permutation(jax.random.fold_in(own, 3), amount)
    donor, taker = mixed[0:amount // 2 * 2:2], mixed[1:amount // 2 * 2:2]
    room = jnp.minimum(tallies[donor] - 1, most - tallies[taker]) // 2
    room = jnp.where((donor == sequence[0]) | (taker == sequence[0]) | (tallies[taker] == 0), 0, jnp.maximum(room, 0))
    passed = jax.random.randint(jax.random.fold_in(own, 4), (amount // 2,), 0, 1 << 20) % (room + 1)
    tallies = tallies.at[donor].add(-passed).at[taker].add(passed)
    labels = jnp.searchsorted(jnp.cumsum(tallies), jnp.arange(rows * top), side="right").astype(jnp.int32)
    grid = labels.reshape(top, rows).T
    grid = grid[jax.random.permutation(jax.random.fold_in(own, 1), rows)]
    rotation = jax.random.randint(jax.random.fold_in(own, 2), (rows, 1), 0, top)
    return jnp.take_along_axis(grid, (jnp.arange(top)[None, :] + rotation) % top, axis=1)


def portions_of(count, total, bound, skew, full):
    portions = [(1 << 20) // math.isqrt(standing ** skew) + 1 for standing in range(1, count + 1)]
    largest = bound if full else min(bound, max(-(-total // count), total * portions[0] // sum(portions)))
    least = 1 if total - largest >= count - 1 else 0
    given, spare = [largest] + [least] * (count - 1), total - largest - least * (count - 1)
    while spare > 0:
        candidates = [i for i in range(1, count) if given[i] < largest] or [i for i in range(1, count) if given[i] < bound]
        mass, budget = sum([portions[i] for i in candidates]), spare
        for i in candidates:
            addition = min(bound - given[i], max(1, budget * portions[i] // mass), spare)
            given[i] = given[i] + addition
            spare = spare - addition
    return np.array(given)


def centred(own_key, shape, spread, limit, cuts=(), dtype=jnp.bfloat16):
    drawn = spread * jax.random.normal(own_key, shape, jnp.float32)
    if cuts:
        drawn = drawn * levels(own_key, shape, cuts, -0.22, 0.18)
    return jnp.clip(drawn, -limit, limit).astype(dtype)


def setup_inputs(seed: int = 0) -> dict:
    seeds = jax.random.split(jax.random.key(seed), 7)
    arrivals = centred(seeds[0], (ROWS, D), 1.0, 6.0, ((0, 256),))
    home_owner_keys = jax.random.split(jax.random.fold_in(seeds[1], 1), ROWS // TOK_DEV)
    home_owner_turns = jax.random.permutation(jax.random.fold_in(seeds[1], 3), ROWS // TOK_DEV)
    home_owner = jax.vmap(lambda own, number: shared_out(jax.random.fold_in(seeds[1], 2), own, number, TOK_DEV, N_OWN, 1, CAP, 2))(home_owner_keys, home_owner_turns).reshape((ROWS, 1))
    cluster_slot = place_ends(jax.random.randint(seeds[2], (ROWS,), 0, CL_DEV), jax.random.fold_in(seeds[2], 1), 0, CL_DEV - 1).astype(jnp.int32)
    bank = centred(seeds[3], (CLUSTERS, BLK, D), 1.0, 6.0, ((0, 64),))
    members = place_ends(jax.random.randint(seeds[4], (CLUSTERS,), 1, BLK + 1), jax.random.fold_in(seeds[4], 1), 1, BLK).astype(jnp.int32)
    centroid_sum = centred(seeds[5], (CLUSTERS, D), 0.2, 1.6, ((0, 64),), jnp.float32)
    return dict(arrivals=arrivals, home_owner=home_owner, cluster_slot=cluster_slot, bank=bank, members=members, centroid_sum=centroid_sum)


epsilon = 1e-06

def reference(arrivals, home_owner, cluster_slot, bank, members, centroid_sum):
    cluster = (home_owner[:, 0] * CL_DEV + cluster_slot).astype(jnp.int32)
    values = arrivals.astype(jnp.float32)
    unit_rows = (values / jnp.sqrt(lax.optimization_barrier(jnp.sum(values * values, axis=1, keepdims=True)) + epsilon)).astype(jnp.bfloat16)

    def block_norms(block_bank):
        widened = block_bank.astype(jnp.float32)
        return jnp.sqrt(lax.optimization_barrier(jnp.sum(widened * widened, axis=2)) + epsilon)
    bank_norm = lax.map(block_norms, bank.reshape(N_OWN, CL_DEV, BLK, D)).reshape(CLUSTERS, BLK)

    def block_best(inputs):
        query, chosen = inputs
        picked = bank[chosen].astype(jnp.float32)
        dot_raw = jnp.einsum('bd,bjd->bj', query.astype(jnp.float32), picked, precision=lax.Precision.HIGHEST)
        cosine = dot_raw / bank_norm[chosen]
        is_valid = jnp.arange(BLK)[None, :] < members[chosen][:, None]
        return lax.optimization_barrier(jnp.max(jnp.where(is_valid, cosine, -3.0), axis=1))
    count_blocks = ROWS // TOK_DEV
    best_cosine = lax.map(block_best, (unit_rows.reshape(count_blocks, TOK_DEV, D), cluster.reshape(count_blocks, TOK_DEV))).reshape(ROWS)
    added = jax.ops.segment_sum(unit_rows.astype(jnp.float32), cluster, num_segments=CLUSTERS)
    total = centroid_sum + added
    centroids = total / jnp.sqrt(lax.optimization_barrier(jnp.sum(total * total, axis=1, keepdims=True)) + epsilon)
    return (best_cosine, centroids)
```

```python
import functools

import jax
import jax.numpy as jnp
from jax import lax
from jax.experimental import pallas as pl
from jax.experimental.pallas import tpu as pltpu
from jax.sharding import PartitionSpec as P

EPS = 1e-06
MESH = pl.DeviceIdType.MESH
Z_ORDER = (4, 0, 3, 5, 2, 6, 1, 7)
SELF_GROUP = Z_ORDER.index(0)
F32, BF16 = jnp.float32, jnp.bfloat16
TILE = 512


def nt(a, b):
    return lax.dot_general(a, b, (((1,), (1,)), ((), ())), preferred_element_type=F32)


def peer(x, z, c, dz, q, sign):
    dx, dc = q // 2, q % 2
    px = lax.rem(x + sign * dx + 4, 4)
    pz = lax.rem(z + sign * dz + 8, 8)
    pc = lax.rem(c + dc, 2)
    return px * 16 + pz * 2 + pc


def kernel(
    arr_h, tgt, slot, bank_h, mem, csum_h, best_o, cent_o,
    arr, bank, rn, colc, kbuf, send, recv, scode, rcode, bests, ret, r8,
    acc, csum, rs_out, rs_in, ag,
    in_sem, bank_sem, self_sem, row_ss, row_rs, code_ss, code_rs, ret_ss, ret_rs,
    rs_ss, rs_rs, ag_ss, ag_rs,
):
    g = lax.axis_index("grp")
    me = lax.axis_index("own")
    x, z, c = me // 16, lax.rem(me // 2, 8), lax.rem(me, 2)
    clusters = mem.shape[0]
    quarter = clusters // 4

    arr_cp = pltpu.make_async_copy(arr_h, arr, in_sem.at[0])
    arr_cp.start()
    csum_cp = pltpu.make_async_copy(
        csum_h.at[pl.ds(g * quarter, quarter), :], csum, in_sem.at[1]
    )
    csum_cp.start()
    bank_cp = pltpu.make_async_copy(bank_h, bank, bank_sem)
    bank_cp.start()

    barrier = pltpu.get_barrier_semaphore()
    for zi, dz in enumerate(Z_ORDER):
        @pl.loop(1 if zi == SELF_GROUP else 0, 8)
        def _(q):
            pl.semaphore_signal(
                barrier, inc=1, device_id=(g, peer(x, z, c, dz, q, 1)), device_id_type=MESH
            )
    for j in range(1, 4):
        pl.semaphore_signal(
            barrier, inc=1, device_id=(lax.rem(g + j, 4), me), device_id_type=MESH
        )

    t = tgt[...]
    dx = ((t >> 4) - x) & 3
    dz = ((t >> 1) - z) & 7
    dc = (t - c) & 1
    zi_of = jnp.zeros_like(t)
    for zi, d in enumerate(Z_ORDER):
        zi_of = jnp.where(dz == d, zi, zi_of)
    pos = zi_of * 8 + dx * 2 + dc
    rows = t.shape[1]
    hit = lax.broadcasted_iota(jnp.int32, (64, rows), 0) == pos
    upper = (
        lax.broadcasted_iota(jnp.int32, (rows, rows), 0)
        < lax.broadcasted_iota(jnp.int32, (rows, rows), 1)
    ).astype(F32).astype(BF16)
    earlier = jnp.dot(hit.astype(F32).astype(BF16), upper, preferred_element_type=F32)
    placed = jnp.sum(jnp.where(hit, earlier, 0.0), axis=0, keepdims=True).astype(jnp.int32)
    k = pos * 16 + placed
    kbuf[...] = k
    code_row = jnp.broadcast_to((slot[...] + 1).astype(F32), (8, rows)).astype(BF16)

    arr_cp.wait()
    values = arr[...].astype(F32)
    unit = (
        values / jnp.sqrt(jnp.sum(values * values, axis=1, keepdims=True) + EPS)
    ).astype(BF16)
    iota128 = lax.broadcasted_iota(jnp.int32, (128, rows), 0)
    for zi in range(8):
        match = (iota128 + zi * 128 == k).astype(F32).astype(BF16)
        send[pl.ds(zi * 8, 8)] = (
            jnp.dot(match, unit, preferred_element_type=F32).astype(BF16).reshape(8, 16, -1)
        )
        scode[zi] = nt(code_row, match)[0:1, :] - 1.0

    pl.semaphore_wait(barrier, 66)

    def row_copy(zi, lo, n, dev):
        part = pl.ds(zi * 8 + lo, n)
        return pltpu.make_async_remote_copy(
            src_ref=send.at[part], dst_ref=recv.at[part], send_sem=row_ss.at[zi],
            recv_sem=row_rs.at[zi], device_id=(g, dev), device_id_type=MESH,
        )

    def code_copy(zi, q, dev):
        return pltpu.make_async_remote_copy(
            src_ref=scode.at[zi], dst_ref=rcode.at[zi * 8 + q], send_sem=code_ss.at[zi],
            recv_sem=code_rs.at[zi], device_id=(g, dev), device_id_type=MESH,
        )

    def ret_copy(zi, q, dev):
        return pltpu.make_async_remote_copy(
            src_ref=bests.at[zi], dst_ref=ret.at[zi * 8 + q], send_sem=ret_ss.at[zi],
            recv_sem=ret_rs.at[zi], device_id=(g, dev), device_id_type=MESH,
        )

    def landed(buf, zi, sem):
        lo = 1 if zi == SELF_GROUP else 0
        part = pl.ds(zi * 8 + lo, 8 - lo)
        return pltpu.make_async_remote_copy(
            src_ref=buf.at[part], dst_ref=buf.at[part], send_sem=sem.at[zi],
            recv_sem=sem.at[zi], device_id=(g, me), device_id_type=MESH,
        )

    me_slot = SELF_GROUP * 8
    self_cp = pltpu.make_async_copy(send.at[me_slot], recv.at[me_slot], self_sem)
    self_cp.start()
    rcode[me_slot] = scode[SELF_GROUP]
    for chunk in range(4):
        @pl.loop(0, 8)
        def _(q):
            for zi in (2 * chunk, 2 * chunk + 1):
                if zi != SELF_GROUP:
                    dev = peer(x, z, c, Z_ORDER[zi], q, 1)
                    code_copy(zi, q, dev).start()
                    row_copy(zi, q, 1, dev).start()
        if SELF_GROUP // 2 == chunk:
            @pl.loop(1, 8)
            def _(q):
                dev = peer(x, z, c, 0, q, 1)
                code_copy(SELF_GROUP, q, dev).start()
                row_copy(SELF_GROUP, q, 1, dev).start()

    @pl.loop(0, clusters)
    def _(cl):
        live = lax.broadcasted_iota(jnp.int32, (32, 128), 0) < mem[cl]
        colc[pl.ds(pl.multiple_of(cl * 32, 32), 32), :] = jnp.where(
            live, jnp.full((32, 128), cl, jnp.int32), -2
        ).astype(F32)

    bank_cp.wait()

    @pl.loop(0, bank.shape[0] // 256)
    def _(i):
        part = pl.ds(pl.multiple_of(i * 256, 256), 256)
        b = bank[part, :].astype(F32)
        norm = 1.0 / jnp.sqrt(jnp.sum(b * b, axis=1, keepdims=True) + EPS)
        rn[part, :] = jnp.broadcast_to(norm, (256, 128))

    lane16 = lax.broadcasted_iota(jnp.int32, (1, 128), 1) // 16

    def folded(buf, zi):
        total = jnp.zeros((1, 128), F32)
        for q in range(8):
            total = jnp.where(lane16 == q, buf[zi * 8 + q], total)
        return total

    def self_lo(zi):
        return 1 if zi == SELF_GROUP else 0

    acc[...] = jnp.zeros_like(acc)
    for chunk in range(4):
        for zi in (2 * chunk, 2 * chunk + 1):
            lo = self_lo(zi)
            landed(recv, zi, row_rs).wait_recv()
            landed(rcode, zi, code_rs).wait_recv()
            if lo:
                self_cp.wait()
        codes = [folded(rcode, zi) for zi in (2 * chunk, 2 * chunk + 1)]
        q_rows = recv[pl.ds(chunk * 16, 16)].reshape(256, -1)
        row_of = jnp.concatenate(codes, axis=1)
        which = (
            lax.broadcasted_iota(jnp.int32, (clusters, 256), 0).astype(F32) == row_of
        ).astype(F32).astype(BF16)
        acc[...] += jnp.dot(which, q_rows, preferred_element_type=F32)
        if chunk == 3:
            for j in range(1, 4):
                to = lax.rem(g + j, 4)
                rs_out[j - 1] = acc[pl.ds(to * quarter, quarter), :]
                rs_copy(g, me, j, rs_out, rs_in, rs_ss, rs_rs).start()

        def tile(i, best):
            part = pl.ds(pl.multiple_of(i * TILE, TILE), TILE)
            s = nt(bank[part, :], q_rows)
            scale, cols = rn[part, :], colc[part, :]
            new = []
            for h in range(2):
                cand = jnp.where(
                    cols == codes[h], s[:, h * 128 : h * 128 + 128] * scale, -3.0
                ).reshape(TILE // 8, 8, 128)
                new.append(jnp.maximum(best[h], jnp.max(cand, axis=0)))
            return tuple(new)

        start = jnp.full((8, 128), -3.0, F32)
        best = lax.fori_loop(0, bank.shape[0] // TILE, tile, (start, start))
        for h in range(2):
            zi = 2 * chunk + h
            bests[zi] = jnp.max(best[h], axis=0, keepdims=True)
            if zi == SELF_GROUP:
                ret[me_slot] = bests[zi]

            @pl.loop(self_lo(zi), 8)
            def _(q):
                ret_copy(zi, q, peer(x, z, c, Z_ORDER[zi], q, -1)).start()

    csum_cp.wait()
    total = csum[...] + acc[pl.ds(g * quarter, quarter), :]
    for j in range(1, 4):
        rs_copy(g, me, j, rs_out, rs_in, rs_ss, rs_rs).wait_recv()
        total += rs_in[j - 1]
    ag[g] = total / jnp.sqrt(jnp.sum(total * total, axis=1, keepdims=True) + EPS)
    for j in range(1, 4):
        ag_copy(g, me, j, ag, ag_ss, ag_rs, g).start()

    for zi in range(8):
        landed(ret, zi, ret_rs).wait_recv()
    for zi in range(8):
        r8[zi : zi + 1, :] = folded(ret, zi)
    k = kbuf[...]
    group = (lax.broadcasted_iota(jnp.int32, (8, rows), 0) == (k >> 7)).astype(F32)
    spread = lax.dot_general(
        r8[...], group, (((0,), (0,)), ((), ())),
        preferred_element_type=F32, precision=lax.Precision.HIGHEST,
    )
    best_o[...] = jnp.sum(
        jnp.where(iota128 == (k & 127), spread, 0.0), axis=0, keepdims=True
    )

    for j in range(1, 4):
        ag_copy(g, me, j, ag, ag_ss, ag_rs, lax.rem(g + 4 - j, 4)).wait_recv()
    cent_o[...] = ag[...].reshape(clusters, -1)

    for zi in range(8):
        landed(send, zi, row_ss).wait_send()
        landed(rcode, zi, code_ss).wait_send()
        landed(ret, zi, ret_ss).wait_send()
    for j in range(1, 4):
        rs_copy(g, me, j, rs_out, rs_in, rs_ss, rs_rs).wait_send()
        ag_copy(g, me, j, ag, ag_ss, ag_rs, g).wait_send()


def rs_copy(g, me, j, rs_out, rs_in, ss, rs):
    return pltpu.make_async_remote_copy(
        src_ref=rs_out.at[j - 1], dst_ref=rs_in.at[j - 1], send_sem=ss.at[j - 1],
        recv_sem=rs.at[j - 1], device_id=(lax.rem(g + j, 4), me), device_id_type=MESH,
    )


def ag_copy(g, me, j, ag, ss, rs, at):
    return pltpu.make_async_remote_copy(
        src_ref=ag.at[at], dst_ref=ag.at[at], send_sem=ss.at[j - 1],
        recv_sem=rs.at[j - 1], device_id=(lax.rem(g + j, 4), me), device_id_type=MESH,
    )


def body(arrivals, home_owner, cluster_slot, bank, members, centroid_sum):
    rows, width = arrivals.shape
    clusters, depth, _ = bank.shape
    dma = pltpu.SemaphoreType.DMA
    hbm = pl.BlockSpec(memory_space=pl.ANY)
    vmem = pl.BlockSpec(memory_space=pltpu.VMEM)
    best, cent = pl.pallas_call(
        kernel,
        out_shape=(
            jax.ShapeDtypeStruct((1, rows), F32),
            jax.ShapeDtypeStruct((clusters, width), F32),
        ),
        in_specs=[hbm, vmem, vmem, hbm, pl.BlockSpec(memory_space=pltpu.SMEM), hbm],
        out_specs=(vmem, vmem),
        scratch_shapes=[
            pltpu.VMEM((rows, width), BF16),
            pltpu.VMEM((clusters * depth, width), BF16),
            pltpu.VMEM((clusters * depth, 128), F32),
            pltpu.VMEM((clusters * depth, 128), F32),
            pltpu.VMEM((1, rows), jnp.int32),
            pltpu.VMEM((64, 16, width), BF16),
            pltpu.VMEM((64, 16, width), BF16),
            pltpu.VMEM((8, 1, 128), F32),
            pltpu.VMEM((64, 1, 128), F32),
            pltpu.VMEM((8, 1, 128), F32),
            pltpu.VMEM((64, 1, 128), F32),
            pltpu.VMEM((8, 128), F32),
            pltpu.VMEM((clusters, width), F32),
            pltpu.VMEM((clusters // 4, width), F32),
            pltpu.VMEM((3, clusters // 4, width), F32),
            pltpu.VMEM((3, clusters // 4, width), F32),
            pltpu.VMEM((4, clusters // 4, width), F32),
            dma((2,)), dma, dma,
            dma((8,)), dma((8,)), dma((8,)), dma((8,)), dma((8,)), dma((8,)),
            dma((3,)), dma((3,)), dma((3,)), dma((3,)),
        ],
        compiler_params=pltpu.CompilerParams(
            collective_id=0, has_side_effects=True, vmem_limit_bytes=56 << 20
        ),
        name="semdedup_round",
    )(
        arrivals,
        home_owner.reshape(1, rows),
        cluster_slot.reshape(1, rows),
        bank.reshape(clusters * depth, width),
        members,
        centroid_sum,
    )
    return best.reshape(rows), cent


def solution(mesh):
    return jax.shard_map(
        body,
        mesh=mesh,
        in_specs=(
            P(("grp", "own"), None),
            P(("grp", "own"), None),
            P(("grp", "own")),
            P("own", None, None),
            P("own"),
            P("own", None),
        ),
        out_specs=(P(("grp", "own")), P("own", None)),
        check_vma=False,
    )
```

```python
import functools

import jax
import jax.numpy as jnp
from jax import lax
from jax.experimental import pallas as pl
from jax.experimental.pallas import tpu as pltpu
from jax.sharding import PartitionSpec as P

EPS = 1e-06
MESH = pl.DeviceIdType.MESH
Z_ORDER = (3, 5, 4, 0, 2, 6, 1, 7)
SELF_GROUP, HALF_RING = Z_ORDER.index(0), Z_ORDER.index(4)
F32, BF16 = jnp.float32, jnp.bfloat16
TILE = 2048


def nt(a, b):
    return lax.dot_general(a, b, (((1,), (1,)), ((), ())), preferred_element_type=F32)


def peer(x, z, c, dz, q, sign):
    dx, dc = q // 2, q % 2
    px = lax.rem(x + sign * dx + 4, 4)
    pz = lax.rem(z + sign * dz + 8, 8)
    pc = lax.rem(c + dc, 2)
    return px * 16 + pz * 2 + pc


def kernel(
    arr_h, tgt, slot, bank_h, mem, csum_h, best_o, cent_o,
    arr, bank, rn, colc, kbuf, send, recv, scode, rcode, bests, ret, r8,
    acc, csum, relay, passed, onward, partial, ag,
    in_sem, bank_sem, self_sem, row_ss, row_rs, code_ss, code_rs, ret_ss, ret_rs,
    relay_sem, rs_ss, rs_rs, ag_ss, ag_rs,
):
    g = lax.axis_index("grp")
    me = lax.axis_index("own")
    x, z, c = me // 16, lax.rem(me // 2, 8), lax.rem(me, 2)
    clusters = mem.shape[0]
    quarter = clusters // 4

    arr_cp = pltpu.make_async_copy(arr_h, arr, in_sem.at[0])
    arr_cp.start()
    csum_cp = pltpu.make_async_copy(
        csum_h.at[pl.ds(g * quarter, quarter), :], csum, in_sem.at[1]
    )
    csum_cp.start()
    bank_cp = pltpu.make_async_copy(bank_h, bank, bank_sem)
    bank_cp.start()

    barrier = pltpu.get_barrier_semaphore()
    for zi, dz in enumerate(Z_ORDER):
        @pl.loop(1 if zi == SELF_GROUP else 0, 8)
        def _(q):
            pl.semaphore_signal(
                barrier, inc=1, device_id=(g, peer(x, z, c, dz, q, 1)), device_id_type=MESH
            )
    for j in range(1, 4):
        pl.semaphore_signal(
            barrier, inc=1, device_id=(lax.rem(g + j, 4), me), device_id_type=MESH
        )

    t = tgt[...]
    dx = ((t >> 4) - x) & 3
    dz = ((t >> 1) - z) & 7
    dc = (t - c) & 1
    zi_of = jnp.zeros_like(t)
    for zi, d in enumerate(Z_ORDER):
        zi_of = jnp.where(dz == d, zi, zi_of)
    pos = zi_of * 8 + dx * 2 + dc
    rows = t.shape[1]
    hit = lax.broadcasted_iota(jnp.int32, (64, rows), 0) == pos
    upper = (
        lax.broadcasted_iota(jnp.int32, (rows, rows), 0)
        < lax.broadcasted_iota(jnp.int32, (rows, rows), 1)
    ).astype(F32).astype(BF16)
    earlier = jnp.dot(hit.astype(F32).astype(BF16), upper, preferred_element_type=F32)
    placed = jnp.sum(jnp.where(hit, earlier, 0.0), axis=0, keepdims=True).astype(jnp.int32)
    k = pos * 16 + placed
    kbuf[...] = k
    code_row = jnp.broadcast_to((slot[...] + 1).astype(F32), (8, rows)).astype(BF16)

    arr_cp.wait()
    values = arr[...].astype(F32)
    unit = (
        values / jnp.sqrt(jnp.sum(values * values, axis=1, keepdims=True) + EPS)
    ).astype(BF16)
    match = (lax.broadcasted_iota(jnp.int32, (1024, rows), 0) == k).astype(F32).astype(BF16)
    send[...] = (
        jnp.dot(match, unit, preferred_element_type=F32).astype(BF16).reshape(64, 16, -1)
    )
    sent_codes = nt(code_row, match)[0:1, :] - 1.0
    for zi in range(8):
        scode[zi] = sent_codes[:, zi * 128 : zi * 128 + 128]

    pl.semaphore_wait(barrier, 66)

    def row_copy(zi, lo, n, dev):
        part = pl.ds(zi * 8 + lo, n)
        return pltpu.make_async_remote_copy(
            src_ref=send.at[part], dst_ref=recv.at[part], send_sem=row_ss.at[zi],
            recv_sem=row_rs.at[zi], device_id=(g, dev), device_id_type=MESH,
        )

    def code_copy(zi, q, dev):
        return pltpu.make_async_remote_copy(
            src_ref=scode.at[zi], dst_ref=rcode.at[zi * 8 + q], send_sem=code_ss.at[zi],
            recv_sem=code_rs.at[zi], device_id=(g, dev), device_id_type=MESH,
        )

    def ret_copy(zi, q, dev):
        return pltpu.make_async_remote_copy(
            src_ref=bests.at[zi], dst_ref=ret.at[zi * 8 + q], send_sem=ret_ss.at[zi],
            recv_sem=ret_rs.at[zi], device_id=(g, dev), device_id_type=MESH,
        )

    def landed(buf, zi, sem):
        lo = 1 if zi == SELF_GROUP else 0
        part = pl.ds(zi * 8 + lo, 8 - lo)
        return pltpu.make_async_remote_copy(
            src_ref=buf.at[part], dst_ref=buf.at[part], send_sem=sem.at[zi],
            recv_sem=sem.at[zi], device_id=(g, me), device_id_type=MESH,
        )

    def piece(far, half):
        start = lax.rem(g + far, 4) * quarter + half * (quarter // 2)
        return pl.ds(pl.multiple_of(start, quarter // 2), quarter // 2)

    def to_next(src, dst, ss, rs, step, side):
        return pltpu.make_async_remote_copy(
            src_ref=src, dst_ref=dst, send_sem=ss.at[step * 2 + side],
            recv_sem=rs.at[step * 2 + side],
            device_id=(lax.rem(g + (1 if side == 0 else 3), 4), me), device_id_type=MESH,
        )

    me_slot = SELF_GROUP * 8
    self_cp = pltpu.make_async_copy(send.at[me_slot], recv.at[me_slot], self_sem)
    self_cp.start()
    rcode[me_slot] = scode[SELF_GROUP]

    def send_rows(zi, q):
        dev = peer(x, z, c, Z_ORDER[zi], q, 1)
        code_copy(zi, q, dev).start()
        row_copy(zi, q, 1, dev).start()

    def first_leg(q, dev):
        return pltpu.make_async_remote_copy(
            src_ref=send.at[HALF_RING * 8 + q], dst_ref=relay.at[q - 4],
            send_sem=row_ss.at[HALF_RING], recv_sem=relay_sem.at[0],
            device_id=(g, dev), device_id_type=MESH,
        )

    def second_leg(dev):
        return pltpu.make_async_remote_copy(
            src_ref=relay, dst_ref=recv.at[pl.ds(HALF_RING * 8 + 4, 4)],
            send_sem=relay_sem.at[1], recv_sem=row_rs.at[HALF_RING],
            device_id=(g, dev), device_id_type=MESH,
        )

    @pl.loop(0, 4)
    def _(q):
        send_rows(HALF_RING, q)
        code_copy(HALF_RING, q + 4, peer(x, z, c, 4, q + 4, 1)).start()
        first_leg(q + 4, peer(x, z, c, 6, q + 4, 1)).start()

    @pl.loop(1, 8)
    def _(q):
        send_rows(SELF_GROUP, q)

    @pl.loop(0, 8)
    def _(q):
        send_rows(0, q)
        send_rows(1, q)

    @pl.loop(0, clusters)
    def _(cl):
        live = lax.broadcasted_iota(jnp.int32, (32, 128), 0) < mem[cl]
        colc[pl.ds(pl.multiple_of(cl * 32, 32), 32), :] = jnp.where(
            live, jnp.full((32, 128), cl, jnp.int32), -2
        ).astype(F32)

    bank_cp.wait()

    @pl.loop(0, bank.shape[0] // 256)
    def _(i):
        part = pl.ds(pl.multiple_of(i * 256, 256), 256)
        b = bank[part, :].astype(F32)
        norm = 1.0 / jnp.sqrt(jnp.sum(b * b, axis=1, keepdims=True) + EPS)
        rn[part, :] = jnp.broadcast_to(norm, (256, 128))

    pltpu.make_async_remote_copy(
        src_ref=relay, dst_ref=relay, send_sem=relay_sem.at[0], recv_sem=relay_sem.at[0],
        device_id=(g, me), device_id_type=MESH,
    ).wait_recv()
    second_leg(peer(x, z, c, 6, 0, 1)).start()

    @pl.loop(0, 8)
    def _(q):
        send_rows(4, q)
        send_rows(5, q)

    @pl.loop(0, 8)
    def _(q):
        send_rows(6, q)
        send_rows(7, q)

    lane16 = lax.broadcasted_iota(jnp.int32, (1, 128), 1) // 16

    def folded(buf, zi):
        total = jnp.zeros((1, 128), F32)
        for q in range(8):
            total = jnp.where(lane16 == q, buf[zi * 8 + q], total)
        return total

    def self_lo(zi):
        return 1 if zi == SELF_GROUP else 0

    acc[...] = jnp.zeros_like(acc)
    for chunk in range(4):
        for zi in (2 * chunk, 2 * chunk + 1):
            lo = self_lo(zi)
            landed(recv, zi, row_rs).wait_recv()
            landed(rcode, zi, code_rs).wait_recv()
            if lo:
                self_cp.wait()
        codes = [folded(rcode, zi) for zi in (2 * chunk, 2 * chunk + 1)]
        q_rows = recv[pl.ds(chunk * 16, 16)].reshape(256, -1)
        row_of = jnp.concatenate(codes, axis=1)
        which = (
            lax.broadcasted_iota(jnp.int32, (clusters, 256), 0).astype(F32) == row_of
        ).astype(F32).astype(BF16)
        acc[...] += jnp.dot(which, q_rows, preferred_element_type=F32)
        if chunk == 3:
            for side in range(2):
                to_next(acc.at[piece(2, side)], passed.at[side], rs_ss, rs_rs, 0, side).start()
            for side in range(2):
                to_next(
                    acc.at[piece(1 if side == 0 else 3, 1 - side)], partial.at[side, 1 - side],
                    rs_ss, rs_rs, 1, side,
                ).start()

        def tile(i, best):
            part = pl.ds(pl.multiple_of(i * TILE, TILE), TILE)
            s = nt(bank[part, :], q_rows)
            scale, cols = rn[part, :], colc[part, :]
            new = []
            for h in range(2):
                cand = jnp.where(
                    cols == codes[h], s[:, h * 128 : h * 128 + 128] * scale, -3.0
                ).reshape(TILE // 8, 8, 128)
                new.append(jnp.maximum(best[h], jnp.max(cand, axis=0)))
            return tuple(new)

        start = jnp.full((8, 128), -3.0, F32)
        best = lax.fori_loop(0, bank.shape[0] // TILE, tile, (start, start))
        for h in range(2):
            zi = 2 * chunk + h
            bests[zi] = jnp.max(best[h], axis=0, keepdims=True)
            if zi == SELF_GROUP:
                ret[me_slot] = bests[zi]

            @pl.loop(self_lo(zi), 8)
            def _(q):
                ret_copy(zi, q, peer(x, z, c, Z_ORDER[zi], q, -1)).start()

    for side in range(2):
        to_next(passed.at[side], passed.at[side], rs_ss, rs_rs, 0, side).wait_recv()
        onward[side] = passed[side] + acc[piece(1 if side == 0 else 3, side)]
        to_next(onward.at[side], partial.at[side, side], rs_ss, rs_rs, 2, side).start()
    csum_cp.wait()
    mine = pl.ds(pl.multiple_of(g * quarter, quarter), quarter)
    total = csum[...] + acc[mine, :]
    for side in range(2):
        for step, half in ((1, 1 - side), (2, side)):
            landing = partial.at[side, half]
            to_next(landing, landing, rs_ss, rs_rs, step, side).wait_recv()
        total += partial[side].reshape(quarter, -1)
    unit_total = total / jnp.sqrt(jnp.sum(total * total, axis=1, keepdims=True) + EPS)
    ag[g] = unit_total.reshape(2, quarter // 2, -1)
    for step in range(2):
        for side in range(2):
            half = ag.at[g, side if step == 0 else 1 - side]
            to_next(half, half, ag_ss, ag_rs, step, side).start()
    for side in range(2):
        half = ag.at[lax.rem(g + 3 + 2 * side, 4), side]
        to_next(half, half, ag_ss, ag_rs, 0, side).wait_recv()
        to_next(half, half, ag_ss, ag_rs, 2, side).start()

    for zi in range(8):
        landed(ret, zi, ret_rs).wait_recv()
    for zi in range(8):
        r8[zi : zi + 1, :] = folded(ret, zi)
    k = kbuf[...]
    group = (lax.broadcasted_iota(jnp.int32, (8, rows), 0) == (k >> 7)).astype(F32)
    lane_of = lax.broadcasted_iota(jnp.int32, (128, rows), 0)
    spread = lax.dot_general(
        r8[...], group, (((0,), (0,)), ((), ())),
        preferred_element_type=F32, precision=lax.Precision.HIGHEST,
    )
    best_o[...] = jnp.sum(
        jnp.where(lane_of == (k & 127), spread, 0.0), axis=0, keepdims=True
    )

    for side in range(2):
        for step, far, half in ((1, 3 + 2 * side, 1 - side), (2, 2, side)):
            landing = ag.at[lax.rem(g + far, 4), half]
            to_next(landing, landing, ag_ss, ag_rs, step, side).wait_recv()
    cent_o[...] = ag[...].reshape(clusters, -1)

    for zi in range(8):
        landed(send, zi, row_ss).wait_send()
        landed(rcode, zi, code_ss).wait_send()
        landed(ret, zi, ret_ss).wait_send()
    second_leg(me).wait_send()
    for step in range(3):
        for side in range(2):
            half = passed.at[side]
            to_next(half, half, rs_ss, rs_rs, step, side).wait_send()
            to_next(half, half, ag_ss, ag_rs, step, side).wait_send()


def body(arrivals, home_owner, cluster_slot, bank, members, centroid_sum):
    rows, width = arrivals.shape
    clusters, depth, _ = bank.shape
    dma = pltpu.SemaphoreType.DMA
    hbm = pl.BlockSpec(memory_space=pl.ANY)
    vmem = pl.BlockSpec(memory_space=pltpu.VMEM)
    best, cent = pl.pallas_call(
        kernel,
        out_shape=(
            jax.ShapeDtypeStruct((1, rows), F32),
            jax.ShapeDtypeStruct((clusters, width), F32),
        ),
        in_specs=[hbm, vmem, vmem, hbm, pl.BlockSpec(memory_space=pltpu.SMEM), hbm],
        out_specs=(vmem, vmem),
        scratch_shapes=[
            pltpu.VMEM((rows, width), BF16),
            pltpu.VMEM((clusters * depth, width), BF16),
            pltpu.VMEM((clusters * depth, 128), F32),
            pltpu.VMEM((clusters * depth, 128), F32),
            pltpu.VMEM((1, rows), jnp.int32),
            pltpu.VMEM((64, 16, width), BF16),
            pltpu.VMEM((64, 16, width), BF16),
            pltpu.VMEM((8, 1, 128), F32),
            pltpu.VMEM((64, 1, 128), F32),
            pltpu.VMEM((8, 1, 128), F32),
            pltpu.VMEM((64, 1, 128), F32),
            pltpu.VMEM((8, 128), F32),
            pltpu.VMEM((clusters, width), F32),
            pltpu.VMEM((clusters // 4, width), F32),
            pltpu.VMEM((4, 16, width), BF16),
            pltpu.VMEM((2, clusters // 8, width), F32),
            pltpu.VMEM((2, clusters // 8, width), F32),
            pltpu.VMEM((2, 2, clusters // 8, width), F32),
            pltpu.VMEM((4, 2, clusters // 8, width), F32),
            dma((2,)), dma, dma,
            dma((8,)), dma((8,)), dma((8,)), dma((8,)), dma((8,)), dma((8,)),
            dma((2,)), dma((6,)), dma((6,)), dma((6,)), dma((6,)),
        ],
        compiler_params=pltpu.CompilerParams(
            collective_id=0, has_side_effects=True, vmem_limit_bytes=56 << 20
        ),
        name="semdedup_round",
    )(
        arrivals,
        home_owner.reshape(1, rows),
        cluster_slot.reshape(1, rows),
        bank.reshape(clusters * depth, width),
        members,
        centroid_sum,
    )
    return best.reshape(rows), cent


def solution(mesh):
    return jax.shard_map(
        body,
        mesh=mesh,
        in_specs=(
            P(("grp", "own"), None),
            P(("grp", "own"), None),
            P(("grp", "own")),
            P("own", None, None),
            P("own"),
            P("own", None),
        ),
        out_specs=(P(("grp", "own")), P("own", None)),
        check_vma=False,
    )
```

```python
import functools

import jax
import jax.numpy as jnp
from jax import lax
from jax.experimental import pallas as pl
from jax.experimental.pallas import tpu as pltpu
from jax.sharding import PartitionSpec as P

EPS = 1e-06
MESH = pl.DeviceIdType.MESH
Z_ORDER = (4, 0, 3, 5, 2, 6, 1, 7)
LINE = (4, 3, 5, 2, 6, 1, 7)
SELF_GROUP = Z_ORDER.index(0)
F32, BF16 = jnp.float32, jnp.bfloat16
TILE = 2048


def nt(a, b):
    return lax.dot_general(a, b, (((1,), (1,)), ((), ())), preferred_element_type=F32)


def peer(x, z, c, dz, q, sign):
    dx, dc = q // 2, q % 2
    px = lax.rem(x + sign * dx + 4, 4)
    pz = lax.rem(z + sign * dz + 8, 8)
    pc = lax.rem(c + dc, 2)
    return px * 16 + pz * 2 + pc


def kernel(
    arr_h, tgt, slot, bank_h, mem, csum_h, best_o, cent_o,
    arr, bank, rn, colc, kbuf, send, recv, scode, rcode, bests, ret, r8,
    acc, csum, passed, onward, partial, ag,
    in_sem, bank_sem, self_sem, row_ss, row_rs, code_ss, code_rs, ret_ss, ret_rs,
    rs_ss, rs_rs, ag_ss, ag_rs, met, out_sem,
):
    g = lax.axis_index("grp")
    me = lax.axis_index("own")
    x, z, c = me // 16, lax.rem(me // 2, 8), lax.rem(me, 2)
    clusters = mem.shape[0]
    quarter = clusters // 4

    arr_cp = pltpu.make_async_copy(arr_h, arr, in_sem.at[0])
    arr_cp.start()
    csum_cp = pltpu.make_async_copy(
        csum_h.at[pl.ds(g * quarter, quarter), :], csum, in_sem.at[1]
    )
    csum_cp.start()
    bank_cp = pltpu.make_async_copy(bank_h, bank, bank_sem)
    bank_cp.start()

    barrier = pltpu.get_barrier_semaphore()
    for dz in LINE:
        pl.semaphore_signal(
            barrier, inc=1, device_id=(g, peer(x, z, c, dz, 0, 1)), device_id_type=MESH
        )
    @pl.loop(1, 8)
    def _(q):
        pl.semaphore_signal(
            barrier, inc=1, device_id=(g, peer(x, z, c, 0, q, 1)), device_id_type=MESH
        )
    for j in range(1, 4):
        pl.semaphore_signal(
            barrier, inc=1, device_id=(lax.rem(g + j, 4), me), device_id_type=MESH
        )

    t = tgt[...]
    dx = ((t >> 4) - x) & 3
    dz = ((t >> 1) - z) & 7
    dc = (t - c) & 1
    zi_of = jnp.zeros_like(t)
    for zi, d in enumerate(Z_ORDER):
        zi_of = jnp.where(dz == d, zi, zi_of)
    pos = zi_of * 8 + dx * 2 + dc
    rows = t.shape[1]
    hit = lax.broadcasted_iota(jnp.int32, (64, rows), 0) == pos
    upper = (
        lax.broadcasted_iota(jnp.int32, (rows, rows), 0)
        < lax.broadcasted_iota(jnp.int32, (rows, rows), 1)
    ).astype(F32).astype(BF16)
    earlier = jnp.dot(hit.astype(F32).astype(BF16), upper, preferred_element_type=F32)
    placed = jnp.sum(jnp.where(hit, earlier, 0.0), axis=0, keepdims=True).astype(jnp.int32)
    k = pos * 16 + placed
    kbuf[...] = k
    code_row = jnp.broadcast_to((slot[...] + 1).astype(F32), (8, rows)).astype(BF16)

    arr_cp.wait()
    values = arr[...].astype(F32)
    unit = (
        values / jnp.sqrt(jnp.sum(values * values, axis=1, keepdims=True) + EPS)
    ).astype(BF16)
    match = (lax.broadcasted_iota(jnp.int32, (1024, rows), 0) == k).astype(F32).astype(BF16)
    send[...] = (
        jnp.dot(match, unit, preferred_element_type=F32).astype(BF16).reshape(64, 16, -1)
    )
    sent_codes = nt(code_row, match)[0:1, :] - 1.0
    for zi in range(8):
        scode[zi] = sent_codes[:, zi * 128 : zi * 128 + 128]

    pl.semaphore_wait(barrier, 17)
    @pl.loop(1, 8)
    def _(q):
        pl.semaphore_signal(
            met, inc=1, device_id=(g, peer(x, z, c, 0, q, 1)), device_id_type=MESH
        )

    def row_copy(zi, lo, n, dev):
        part = pl.ds(zi * 8 + lo, n)
        return pltpu.make_async_remote_copy(
            src_ref=send.at[part], dst_ref=recv.at[part], send_sem=row_ss.at[zi],
            recv_sem=row_rs.at[zi], device_id=(g, dev), device_id_type=MESH,
        )

    def code_copy(zi, q, dev):
        return pltpu.make_async_remote_copy(
            src_ref=scode.at[zi], dst_ref=rcode.at[zi * 8 + q], send_sem=code_ss.at[zi],
            recv_sem=code_rs.at[zi], device_id=(g, dev), device_id_type=MESH,
        )

    def ret_copy(zi, q, dev):
        return pltpu.make_async_remote_copy(
            src_ref=bests.at[zi], dst_ref=ret.at[zi * 8 + q], send_sem=ret_ss.at[zi],
            recv_sem=ret_rs.at[zi], device_id=(g, dev), device_id_type=MESH,
        )

    def landed(buf, zi, sem):
        lo = 1 if zi == SELF_GROUP else 0
        part = pl.ds(zi * 8 + lo, 8 - lo)
        return pltpu.make_async_remote_copy(
            src_ref=buf.at[part], dst_ref=buf.at[part], send_sem=sem.at[zi],
            recv_sem=sem.at[zi], device_id=(g, me), device_id_type=MESH,
        )

    def piece(far, half):
        start = lax.rem(g + far, 4) * quarter + half * (quarter // 2)
        return pl.ds(pl.multiple_of(start, quarter // 2), quarter // 2)

    def to_next(src, dst, ss, rs, step, side):
        return pltpu.make_async_remote_copy(
            src_ref=src, dst_ref=dst, send_sem=ss.at[step * 2 + side],
            recv_sem=rs.at[step * 2 + side],
            device_id=(lax.rem(g + (1 if side == 0 else 3), 4), me), device_id_type=MESH,
        )

    me_slot = SELF_GROUP * 8
    self_cp = pltpu.make_async_copy(send.at[me_slot], recv.at[me_slot], self_sem)
    self_cp.start()
    rcode[me_slot] = scode[SELF_GROUP]

    def send_rows(zi, q):
        dev = peer(x, z, c, Z_ORDER[zi], q, 1)
        code_copy(zi, q, dev).start()
        row_copy(zi, q, 1, dev).start()

    for dz in LINE:
        send_rows(Z_ORDER.index(dz), 0)

    @pl.loop(1, 8)
    def _(q):
        send_rows(SELF_GROUP, q)

    pl.semaphore_wait(met, 7)

    for pair in ((4,), (3, 5), (2, 6), (1, 7)):
        @pl.loop(1, 8)
        def _(q):
            for dz in pair:
                send_rows(Z_ORDER.index(dz), q)

    @pl.loop(0, clusters)
    def _(cl):
        live = lax.broadcasted_iota(jnp.int32, (32, 128), 0) < mem[cl]
        colc[pl.ds(pl.multiple_of(cl * 32, 32), 32), :] = jnp.where(
            live, jnp.full((32, 128), cl, jnp.int32), -2
        ).astype(F32)

    bank_cp.wait()

    @pl.loop(0, bank.shape[0] // 256)
    def _(i):
        part = pl.ds(pl.multiple_of(i * 256, 256), 256)
        b = bank[part, :].astype(F32)
        norm = 1.0 / jnp.sqrt(jnp.sum(b * b, axis=1, keepdims=True) + EPS)
        rn[part, :] = jnp.broadcast_to(norm, (256, 128))

    lane16 = lax.broadcasted_iota(jnp.int32, (1, 128), 1) // 16

    def folded(buf, zi):
        total = jnp.zeros((1, 128), F32)
        for q in range(8):
            total = jnp.where(lane16 == q, buf[zi * 8 + q], total)
        return total

    def self_lo(zi):
        return 1 if zi == SELF_GROUP else 0

    acc[...] = jnp.zeros_like(acc)
    for chunk in range(4):
        for zi in (2 * chunk, 2 * chunk + 1):
            lo = self_lo(zi)
            landed(recv, zi, row_rs).wait_recv()
            landed(rcode, zi, code_rs).wait_recv()
            if lo:
                self_cp.wait()
        codes = [folded(rcode, zi) for zi in (2 * chunk, 2 * chunk + 1)]
        q_rows = recv[pl.ds(chunk * 16, 16)].reshape(256, -1)
        row_of = jnp.concatenate(codes, axis=1)
        which = (
            lax.broadcasted_iota(jnp.int32, (clusters, 256), 0).astype(F32) == row_of
        ).astype(F32).astype(BF16)
        acc[...] += jnp.dot(which, q_rows, preferred_element_type=F32)
        if chunk == 3:
            for side in range(2):
                to_next(acc.at[piece(2, side)], passed.at[side], rs_ss, rs_rs, 0, side).start()

        def tile(i, best):
            part = pl.ds(pl.multiple_of(i * TILE, TILE), TILE)
            s = nt(bank[part, :], q_rows)
            scale, cols = rn[part, :], colc[part, :]
            new = []
            for h in range(2):
                cand = jnp.where(
                    cols == codes[h], s[:, h * 128 : h * 128 + 128] * scale, -3.0
                ).reshape(TILE // 8, 8, 128)
                new.append(jnp.maximum(best[h], jnp.max(cand, axis=0)))
            return tuple(new)

        start = jnp.full((8, 128), -3.0, F32)
        tiles = bank.shape[0] // TILE
        if chunk < 3:
            best = lax.fori_loop(0, tiles, tile, (start, start))
        else:
            best = tile(0, (start, start))
            for side in range(2):
                to_next(
                    acc.at[piece(1 if side == 0 else 3, 1 - side)], partial.at[side, 1 - side],
                    rs_ss, rs_rs, 1, side,
                ).start()
            best = lax.fori_loop(1, tiles - 1, tile, best)
            for side in range(2):
                to_next(passed.at[side], passed.at[side], rs_ss, rs_rs, 0, side).wait_recv()
                onward[side] = passed[side] + acc[piece(1 if side == 0 else 3, side)]
                to_next(onward.at[side], partial.at[side, side], rs_ss, rs_rs, 2, side).start()
            best = tile(tiles - 1, best)
        for h in range(2):
            zi = 2 * chunk + h
            bests[zi] = jnp.max(best[h], axis=0, keepdims=True)
            if zi == SELF_GROUP:
                ret[me_slot] = bests[zi]

            @pl.loop(self_lo(zi), 8)
            def _(q):
                ret_copy(zi, q, peer(x, z, c, Z_ORDER[zi], q, -1)).start()

    csum_cp.wait()
    mine = pl.ds(pl.multiple_of(g * quarter, quarter), quarter)
    total = csum[...] + acc[mine, :]
    for side in range(2):
        for step, half in ((1, 1 - side), (2, side)):
            landing = partial.at[side, half]
            to_next(landing, landing, rs_ss, rs_rs, step, side).wait_recv()
        total += partial[side].reshape(quarter, -1)
    unit_total = total / jnp.sqrt(jnp.sum(total * total, axis=1, keepdims=True) + EPS)
    ag[g] = unit_total.reshape(2, quarter // 2, -1)

    def publish(far, half):
        at = lax.rem(g + far, 4)
        return pltpu.make_async_copy(
            ag.at[at, half], cent_o.at[at, half], out_sem.at[far * 2 + half]
        )

    def spread_mine(step):
        for side in range(2):
            half = ag.at[g, side if step == 0 else 1 - side]
            to_next(half, half, ag_ss, ag_rs, step, side).start()
            if step == 0:
                publish(0, side).start()

    spread_mine(0)

    for side in range(2):
        half = ag.at[g, side]
        to_next(half, half, ag_ss, ag_rs, 0, side).wait_send()
    spread_mine(1)
    for side in range(2):
        half = ag.at[lax.rem(g + 3 + 2 * side, 4), side]
        to_next(half, half, ag_ss, ag_rs, 0, side).wait_recv()
        to_next(half, half, ag_ss, ag_rs, 2, side).start()
        publish(3 if side == 0 else 1, side).start()

    for zi in range(8):
        landed(ret, zi, ret_rs).wait_recv()
    for zi in range(8):
        r8[zi : zi + 1, :] = folded(ret, zi)
    k = kbuf[...]
    group = (lax.broadcasted_iota(jnp.int32, (8, rows), 0) == (k >> 7)).astype(F32)
    lane_of = lax.broadcasted_iota(jnp.int32, (128, rows), 0)
    spread = lax.dot_general(
        r8[...], group, (((0,), (0,)), ((), ())),
        preferred_element_type=F32, precision=lax.Precision.HIGHEST,
    )
    best_o[...] = jnp.sum(
        jnp.where(lane_of == (k & 127), spread, 0.0), axis=0, keepdims=True
    )

    for side in range(2):
        for step, far, half in ((1, 3 - 2 * side, 1 - side), (2, 2, side)):
            landing = ag.at[lax.rem(g + far, 4), half]
            to_next(landing, landing, ag_ss, ag_rs, step, side).wait_recv()
            publish(far, half).start()
    for far in range(4):
        for half in range(2):
            publish(far, half).wait()

    for zi in range(8):
        landed(send, zi, row_ss).wait_send()
        landed(rcode, zi, code_ss).wait_send()
        landed(ret, zi, ret_ss).wait_send()
    for step in range(3):
        for side in range(2):
            half = passed.at[side]
            to_next(half, half, rs_ss, rs_rs, step, side).wait_send()
            if step > 0:
                to_next(half, half, ag_ss, ag_rs, step, side).wait_send()


def body(arrivals, home_owner, cluster_slot, bank, members, centroid_sum):
    rows, width = arrivals.shape
    clusters, depth, _ = bank.shape
    dma = pltpu.SemaphoreType.DMA
    hbm = pl.BlockSpec(memory_space=pl.ANY)
    vmem = pl.BlockSpec(memory_space=pltpu.VMEM)
    best, cent = pl.pallas_call(
        kernel,
        out_shape=(
            jax.ShapeDtypeStruct((1, rows), F32),
            jax.ShapeDtypeStruct((4, 2, clusters // 8, width), F32),
        ),
        in_specs=[hbm, vmem, vmem, hbm, pl.BlockSpec(memory_space=pltpu.SMEM), hbm],
        out_specs=(vmem, hbm),
        scratch_shapes=[
            pltpu.VMEM((rows, width), BF16),
            pltpu.VMEM((clusters * depth, width), BF16),
            pltpu.VMEM((clusters * depth, 128), F32),
            pltpu.VMEM((clusters * depth, 128), F32),
            pltpu.VMEM((1, rows), jnp.int32),
            pltpu.VMEM((64, 16, width), BF16),
            pltpu.VMEM((64, 16, width), BF16),
            pltpu.VMEM((8, 1, 128), F32),
            pltpu.VMEM((64, 1, 128), F32),
            pltpu.VMEM((8, 1, 128), F32),
            pltpu.VMEM((64, 1, 128), F32),
            pltpu.VMEM((8, 128), F32),
            pltpu.VMEM((clusters, width), F32),
            pltpu.VMEM((clusters // 4, width), F32),
            pltpu.VMEM((2, clusters // 8, width), F32),
            pltpu.VMEM((2, clusters // 8, width), F32),
            pltpu.VMEM((2, 2, clusters // 8, width), F32),
            pltpu.VMEM((4, 2, clusters // 8, width), F32),
            dma((2,)), dma, dma,
            dma((8,)), dma((8,)), dma((8,)), dma((8,)), dma((8,)), dma((8,)),
            dma((6,)), dma((6,)), dma((6,)), dma((6,)),
            pltpu.SemaphoreType.REGULAR, dma((8,)),
        ],
        compiler_params=pltpu.CompilerParams(
            collective_id=0, has_side_effects=True, vmem_limit_bytes=56 << 20
        ),
        name="semdedup_round",
    )(
        arrivals,
        home_owner.reshape(1, rows),
        cluster_slot.reshape(1, rows),
        bank.reshape(clusters * depth, width),
        members,
        centroid_sum,
    )
    return best.reshape(rows), cent.reshape(clusters, width)


def solution(mesh):
    return jax.shard_map(
        body,
        mesh=mesh,
        in_specs=(
            P(("grp", "own"), None),
            P(("grp", "own"), None),
            P(("grp", "own")),
            P("own", None, None),
            P("own"),
            P("own", None),
        ),
        out_specs=(P(("grp", "own")), P("own", None)),
        check_vma=False,
    )
```

```python
import functools

import jax
import jax.numpy as jnp
from jax import lax
from jax.experimental import pallas as pl
from jax.experimental.pallas import tpu as pltpu
from jax.sharding import PartitionSpec as P

EPS = 1e-06
MESH = pl.DeviceIdType.MESH
Z_ORDER = (4, 0, 3, 5, 2, 6, 1, 7)
LINE = (4, 3, 5, 2, 6, 1, 7)
SELF_GROUP = Z_ORDER.index(0)
F32, BF16 = jnp.float32, jnp.bfloat16
TILE = 2048


def nt(a, b):
    return lax.dot_general(a, b, (((1,), (1,)), ((), ())), preferred_element_type=F32)


def peer(x, z, c, dz, q, sign):
    dx, dc = q // 2, q % 2
    px = lax.rem(x + sign * dx + 4, 4)
    pz = lax.rem(z + sign * dz + 8, 8)
    pc = lax.rem(c + dc, 2)
    return px * 16 + pz * 2 + pc


def kernel(
    arr_h, tgt_h, slot_h, bank_h, mem_h, csum_h, best_o, cent_o,
    tgt, slot, mem, arr, bank, rn, colc, kbuf, send, recv, scode, zcode, rcode, bests, ret, r8,
    acc, csum, passed, onward, partial, ag,
    in_sem, bank_sem, self_sem, row_ss, row_rs, code_ss, code_rs, ret_ss, ret_rs,
    rs_ss, rs_rs, ag_ss, ag_rs, met, out_sem,
):
    g = lax.axis_index("grp")
    me = lax.axis_index("own")
    x, z, c = me // 16, lax.rem(me // 2, 8), lax.rem(me, 2)
    clusters = mem_h.shape[0]
    quarter = clusters // 4

    barrier = pltpu.get_barrier_semaphore()
    for dz in LINE:
        pl.semaphore_signal(
            barrier, inc=1, device_id=(g, peer(x, z, c, dz, 0, 1)), device_id_type=MESH
        )
    @pl.loop(1, 8)
    def _(q):
        pl.semaphore_signal(
            barrier, inc=1, device_id=(g, peer(x, z, c, 0, q, 1)), device_id_type=MESH
        )
    for j in range(1, 4):
        pl.semaphore_signal(
            barrier, inc=1, device_id=(lax.rem(g + j, 4), me), device_id_type=MESH
        )

    tgt_cp = pltpu.make_async_copy(tgt_h, tgt, in_sem.at[2])
    tgt_cp.start()
    slot_cp = pltpu.make_async_copy(slot_h, slot, in_sem.at[3])
    slot_cp.start()
    arr_cp = pltpu.make_async_copy(arr_h, arr, in_sem.at[0])
    arr_cp.start()
    csum_cp = pltpu.make_async_copy(
        csum_h.at[pl.ds(g * quarter, quarter), :], csum, in_sem.at[1]
    )
    csum_cp.start()
    bank_cp = pltpu.make_async_copy(bank_h, bank, bank_sem)
    bank_cp.start()
    mem_cp = pltpu.make_async_copy(mem_h, mem, in_sem.at[4])
    mem_cp.start()

    tgt_cp.wait()
    t = tgt[...]
    dx = ((t >> 4) - x) & 3
    dz = ((t >> 1) - z) & 7
    dc = (t - c) & 1
    zi_of = jnp.zeros_like(t)
    for zi, d in enumerate(Z_ORDER):
        zi_of = jnp.where(dz == d, zi, zi_of)
    pos = zi_of * 8 + dx * 2 + dc
    rows = t.shape[1]
    hit = lax.broadcasted_iota(jnp.int32, (64, rows), 0) == pos
    upper = (
        lax.broadcasted_iota(jnp.int32, (rows, rows), 0)
        < lax.broadcasted_iota(jnp.int32, (rows, rows), 1)
    ).astype(F32).astype(BF16)
    earlier = jnp.dot(hit.astype(F32).astype(BF16), upper, preferred_element_type=F32)
    placed = jnp.sum(jnp.where(hit, earlier, 0.0), axis=0, keepdims=True).astype(jnp.int32)
    k = pos * 16 + placed
    kbuf[...] = k
    slot_cp.wait()
    code_row = jnp.broadcast_to((slot[...] + 1).astype(F32), (8, rows)).astype(BF16)

    arr_cp.wait()
    values = arr[...].astype(F32)
    unit = (
        values / jnp.sqrt(jnp.sum(values * values, axis=1, keepdims=True) + EPS)
    ).astype(BF16)
    match = (lax.broadcasted_iota(jnp.int32, (1024, rows), 0) == k).astype(F32).astype(BF16)
    send[...] = (
        jnp.dot(match, unit, preferred_element_type=F32).astype(BF16).reshape(64, 16, -1)
    )
    sent_codes = nt(code_row, match)[0:1, :] - 1.0
    for zi in range(8):
        scode[zi] = sent_codes[:, zi * 128 : zi * 128 + 128]

    pl.semaphore_wait(barrier, 17)
    @pl.loop(1, 8)
    def _(q):
        pl.semaphore_signal(
            met, inc=1, device_id=(g, peer(x, z, c, 0, q, 1)), device_id_type=MESH
        )

    def row_copy(zi, lo, n, dev):
        part = pl.ds(zi * 8 + lo, n)
        return pltpu.make_async_remote_copy(
            src_ref=send.at[part], dst_ref=recv.at[part], send_sem=row_ss.at[zi],
            recv_sem=row_rs.at[zi], device_id=(g, dev), device_id_type=MESH,
        )

    def code_z(zi):
        return pltpu.make_async_remote_copy(
            src_ref=scode.at[zi], dst_ref=zcode.at[zi], send_sem=code_ss.at[zi],
            recv_sem=code_rs.at[zi], device_id=(g, peer(x, z, c, Z_ORDER[zi], 0, 1)),
            device_id_type=MESH,
        )

    def code_x(q, dev):
        return pltpu.make_async_remote_copy(
            src_ref=zcode, dst_ref=rcode.at[q], send_sem=code_ss.at[SELF_GROUP],
            recv_sem=code_rs.at[SELF_GROUP], device_id=(g, dev), device_id_type=MESH,
        )

    def codes_x():
        return pltpu.make_async_remote_copy(
            src_ref=rcode.at[pl.ds(1, 7)], dst_ref=rcode.at[pl.ds(1, 7)],
            send_sem=code_ss.at[SELF_GROUP], recv_sem=code_rs.at[SELF_GROUP],
            device_id=(g, me), device_id_type=MESH,
        )

    def ret_copy(zi, q, dev):
        return pltpu.make_async_remote_copy(
            src_ref=bests.at[zi], dst_ref=ret.at[zi * 8 + q], send_sem=ret_ss.at[zi],
            recv_sem=ret_rs.at[zi], device_id=(g, dev), device_id_type=MESH,
        )

    def landed(buf, zi, sem):
        lo = 1 if zi == SELF_GROUP else 0
        part = pl.ds(zi * 8 + lo, 8 - lo)
        return pltpu.make_async_remote_copy(
            src_ref=buf.at[part], dst_ref=buf.at[part], send_sem=sem.at[zi],
            recv_sem=sem.at[zi], device_id=(g, me), device_id_type=MESH,
        )

    def piece(far, half):
        start = lax.rem(g + far, 4) * quarter + half * (quarter // 2)
        return pl.ds(pl.multiple_of(start, quarter // 2), quarter // 2)

    def to_next(src, dst, ss, rs, step, side):
        return pltpu.make_async_remote_copy(
            src_ref=src, dst_ref=dst, send_sem=ss.at[step * 2 + side],
            recv_sem=rs.at[step * 2 + side],
            device_id=(lax.rem(g + (1 if side == 0 else 3), 4), me), device_id_type=MESH,
        )

    me_slot = SELF_GROUP * 8
    self_cp = pltpu.make_async_copy(send.at[me_slot], recv.at[me_slot], self_sem)
    self_cp.start()
    zcode[SELF_GROUP] = scode[SELF_GROUP]

    def send_rows(zi, q):
        dev = peer(x, z, c, Z_ORDER[zi], q, 1)
        row_copy(zi, q, 1, dev).start()

    for dz in LINE:
        code_z(Z_ORDER.index(dz)).start()
        send_rows(Z_ORDER.index(dz), 0)

    @pl.loop(1, 8)
    def _(q):
        send_rows(SELF_GROUP, q)

    pl.semaphore_wait(met, 7)

    for pair in ((4,), (3, 5), (2, 6), (1, 7)):
        @pl.loop(1, 8)
        def _(q):
            for dz in pair:
                send_rows(Z_ORDER.index(dz), q)

    mem_cp.wait()
    @pl.loop(0, clusters)
    def _(cl):
        live = lax.broadcasted_iota(jnp.int32, (32, 128), 0) < mem[cl]
        colc[pl.ds(pl.multiple_of(cl * 32, 32), 32), :] = jnp.where(
            live, jnp.full((32, 128), cl, jnp.int32), -2
        ).astype(F32)

    bank_cp.wait()

    @pl.loop(0, bank.shape[0] // 256)
    def _(i):
        part = pl.ds(pl.multiple_of(i * 256, 256), 256)
        b = bank[part, :].astype(F32)
        norm = 1.0 / jnp.sqrt(jnp.sum(b * b, axis=1, keepdims=True) + EPS)
        rn[part, :] = jnp.broadcast_to(norm, (256, 128))

    for dz in LINE:
        code_z(Z_ORDER.index(dz)).wait_recv()
    rcode[0] = zcode[...]

    @pl.loop(1, 8)
    def _(q):
        code_x(q, peer(x, z, c, 0, q, 1)).start()

    lane16 = lax.broadcasted_iota(jnp.int32, (1, 128), 1) // 16

    def folded(parts):
        total = jnp.zeros((1, 128), F32)
        for q in range(8):
            total = jnp.where(lane16 == q, parts[q], total)
        return total

    def self_lo(zi):
        return 1 if zi == SELF_GROUP else 0

    acc[...] = jnp.zeros_like(acc)
    for chunk in range(4):
        for zi in (2 * chunk, 2 * chunk + 1):
            lo = self_lo(zi)
            landed(recv, zi, row_rs).wait_recv()
            if lo:
                self_cp.wait()
        if chunk == 0:
            codes_x().wait_recv()
        codes = [
            folded([rcode[q, zi] for q in range(8)]) for zi in (2 * chunk, 2 * chunk + 1)
        ]
        q_rows = recv[pl.ds(chunk * 16, 16)].reshape(256, -1)
        row_of = jnp.concatenate(codes, axis=1)
        which = (
            lax.broadcasted_iota(jnp.int32, (clusters, 256), 0).astype(F32) == row_of
        ).astype(F32).astype(BF16)
        acc[...] += jnp.dot(which, q_rows, preferred_element_type=F32)
        if chunk == 3:
            for side in range(2):
                to_next(acc.at[piece(2, side)], passed.at[side], rs_ss, rs_rs, 0, side).start()

        def tile(i, best):
            part = pl.ds(pl.multiple_of(i * TILE, TILE), TILE)
            s = nt(bank[part, :], q_rows)
            scale, cols = rn[part, :], colc[part, :]
            new = []
            for h in range(2):
                cand = jnp.where(
                    cols == codes[h], s[:, h * 128 : h * 128 + 128] * scale, -3.0
                ).reshape(TILE // 8, 8, 128)
                new.append(jnp.maximum(best[h], jnp.max(cand, axis=0)))
            return tuple(new)

        start = jnp.full((8, 128), -3.0, F32)
        tiles = bank.shape[0] // TILE
        if chunk < 3:
            best = lax.fori_loop(0, tiles, tile, (start, start))
        else:
            best = tile(0, (start, start))
            for side in range(2):
                to_next(
                    acc.at[piece(1 if side == 0 else 3, 1 - side)], partial.at[side, 1 - side],
                    rs_ss, rs_rs, 1, side,
                ).start()
            best = lax.fori_loop(1, tiles - 1, tile, best)
            for side in range(2):
                to_next(passed.at[side], passed.at[side], rs_ss, rs_rs, 0, side).wait_recv()
                onward[side] = passed[side] + acc[piece(1 if side == 0 else 3, side)]
                to_next(onward.at[side], partial.at[side, side], rs_ss, rs_rs, 2, side).start()
            best = tile(tiles - 1, best)
        for h in range(2):
            zi = 2 * chunk + h
            bests[zi] = jnp.max(best[h], axis=0, keepdims=True)
            if zi == SELF_GROUP:
                ret[me_slot] = bests[zi]

    for zi in range(8):
        @pl.loop(self_lo(zi), 8)
        def _(q):
            ret_copy(zi, q, peer(x, z, c, Z_ORDER[zi], q, -1)).start()

    csum_cp.wait()
    mine = pl.ds(pl.multiple_of(g * quarter, quarter), quarter)
    total = csum[...] + acc[mine, :]
    for side in range(2):
        for step, half in ((1, 1 - side), (2, side)):
            landing = partial.at[side, half]
            to_next(landing, landing, rs_ss, rs_rs, step, side).wait_recv()
        total += partial[side].reshape(quarter, -1)
    unit_total = total / jnp.sqrt(jnp.sum(total * total, axis=1, keepdims=True) + EPS)
    ag[g] = unit_total.reshape(2, quarter // 2, -1)

    def publish(far, half):
        at = lax.rem(g + far, 4)
        return pltpu.make_async_copy(
            ag.at[at, half], cent_o.at[at, half], out_sem.at[far * 2 + half]
        )

    def spread_mine(step):
        for side in range(2):
            half = ag.at[g, side if step == 0 else 1 - side]
            to_next(half, half, ag_ss, ag_rs, step, side).start()
            if step == 0:
                publish(0, side).start()

    spread_mine(0)

    for side in range(2):
        half = ag.at[g, side]
        to_next(half, half, ag_ss, ag_rs, 0, side).wait_send()
    spread_mine(1)
    for side in range(2):
        half = ag.at[lax.rem(g + 3 + 2 * side, 4), side]
        to_next(half, half, ag_ss, ag_rs, 0, side).wait_recv()
        to_next(half, half, ag_ss, ag_rs, 2, side).start()
        publish(3 if side == 0 else 1, side).start()

    for zi in range(8):
        landed(ret, zi, ret_rs).wait_recv()
    for zi in range(8):
        r8[zi : zi + 1, :] = folded([ret[zi * 8 + q] for q in range(8)])
    k = kbuf[...]
    group = (lax.broadcasted_iota(jnp.int32, (8, rows), 0) == (k >> 7)).astype(F32)
    lane_of = lax.broadcasted_iota(jnp.int32, (128, rows), 0)
    spread = lax.dot_general(
        r8[...], group, (((0,), (0,)), ((), ())),
        preferred_element_type=F32, precision=lax.Precision.HIGHEST,
    )
    best_o[...] = jnp.sum(
        jnp.where(lane_of == (k & 127), spread, 0.0), axis=0, keepdims=True
    )

    for side in range(2):
        for step, far, half in ((1, 3 - 2 * side, 1 - side), (2, 2, side)):
            landing = ag.at[lax.rem(g + far, 4), half]
            to_next(landing, landing, ag_ss, ag_rs, step, side).wait_recv()
            publish(far, half).start()
    for far in range(4):
        for half in range(2):
            publish(far, half).wait()

    for zi in range(8):
        landed(send, zi, row_ss).wait_send()
        landed(ret, zi, ret_ss).wait_send()
    for dz in LINE:
        code_z(Z_ORDER.index(dz)).wait_send()
    codes_x().wait_send()
    for step in range(3):
        for side in range(2):
            half = passed.at[side]
            to_next(half, half, rs_ss, rs_rs, step, side).wait_send()
            if step > 0:
                to_next(half, half, ag_ss, ag_rs, step, side).wait_send()


def hand_on(best_i, cent_i, best_o, cent_o, best_v, cent_v, sem):
    first = [
        pltpu.make_async_copy(best_i, best_v, sem.at[0]),
        pltpu.make_async_copy(cent_i, cent_v, sem.at[1]),
    ]
    for copy in first:
        copy.start()
    second = [
        pltpu.make_async_copy(best_v, best_o, sem.at[2]),
        pltpu.make_async_copy(cent_v, cent_o, sem.at[3]),
    ]
    for before, after in zip(first, second):
        before.wait()
        after.start()
    for copy in second:
        copy.wait()


def body(arrivals, home_owner, cluster_slot, bank, members, centroid_sum):
    rows, width = arrivals.shape
    clusters, depth, _ = bank.shape
    dma = pltpu.SemaphoreType.DMA
    hbm = pl.BlockSpec(memory_space=pl.ANY)
    vmem = pl.BlockSpec(memory_space=pltpu.VMEM)
    best, cent = pl.pallas_call(
        kernel,
        out_shape=(
            jax.ShapeDtypeStruct((1, rows), F32),
            jax.ShapeDtypeStruct((4, 2, clusters // 8, width), F32),
        ),
        in_specs=[hbm] * 6,
        out_specs=(vmem, hbm),
        scratch_shapes=[
            pltpu.VMEM((1, rows), jnp.int32),
            pltpu.VMEM((1, rows), jnp.int32),
            pltpu.SMEM((clusters,), jnp.int32),
            pltpu.VMEM((rows, width), BF16),
            pltpu.VMEM((clusters * depth, width), BF16),
            pltpu.VMEM((clusters * depth, 128), F32),
            pltpu.VMEM((clusters * depth, 128), F32),
            pltpu.VMEM((1, rows), jnp.int32),
            pltpu.VMEM((64, 16, width), BF16),
            pltpu.VMEM((64, 16, width), BF16),
            pltpu.VMEM((8, 1, 128), F32),
            pltpu.VMEM((8, 1, 128), F32),
            pltpu.VMEM((8, 8, 1, 128), F32),
            pltpu.VMEM((8, 1, 128), F32),
            pltpu.VMEM((64, 1, 128), F32),
            pltpu.VMEM((8, 128), F32),
            pltpu.VMEM((clusters, width), F32),
            pltpu.VMEM((clusters // 4, width), F32),
            pltpu.VMEM((2, clusters // 8, width), F32),
            pltpu.VMEM((2, clusters // 8, width), F32),
            pltpu.VMEM((2, 2, clusters // 8, width), F32),
            pltpu.VMEM((4, 2, clusters // 8, width), F32),
            dma((5,)), dma, dma,
            dma((8,)), dma((8,)), dma((8,)), dma((8,)), dma((8,)), dma((8,)),
            dma((6,)), dma((6,)), dma((6,)), dma((6,)),
            pltpu.SemaphoreType.REGULAR, dma((8,)),
        ],
        compiler_params=pltpu.CompilerParams(
            collective_id=0, has_side_effects=True, vmem_limit_bytes=56 << 20
        ),
        name="semdedup_round",
    )(
        arrivals,
        home_owner.reshape(1, rows),
        cluster_slot.reshape(1, rows),
        bank.reshape(clusters * depth, width),
        members,
        centroid_sum,
    )
    best, cent = pl.pallas_call(
        hand_on,
        out_shape=(
            jax.ShapeDtypeStruct(best.shape, F32), jax.ShapeDtypeStruct(cent.shape, F32)
        ),
        in_specs=[hbm, hbm],
        out_specs=(hbm, hbm),
        scratch_shapes=[pltpu.VMEM(best.shape, F32), pltpu.VMEM(cent.shape, F32), dma((4,))],
        name="hand_on",
    )(best, cent)
    return best.reshape(rows), cent.reshape(clusters, width)


def solution(mesh):
    return jax.shard_map(
        body,
        mesh=mesh,
        in_specs=(
            P(("grp", "own"), None),
            P(("grp", "own"), None),
            P(("grp", "own")),
            P("own", None, None),
            P("own"),
            P("own", None),
        ),
        out_specs=(P(("grp", "own")), P("own", None)),
        check_vma=False,
    )
```

```python
import functools

import jax
import jax.numpy as jnp
from jax import lax
from jax.experimental import pallas as pl
from jax.experimental.pallas import tpu as pltpu
from jax.sharding import PartitionSpec as P

EPS = 1e-06
MESH = pl.DeviceIdType.MESH
Z_ORDER = (4, 0, 3, 5, 2, 6, 1, 7)
LINE = (4, 3, 5, 2, 6, 1, 7)
SELF_GROUP = Z_ORDER.index(0)
F32, BF16 = jnp.float32, jnp.bfloat16
TILE = 2048
FACTOR, DEFER = 1, 1


def nt(a, b):
    return lax.dot_general(a, b, (((1,), (1,)), ((), ())), preferred_element_type=F32)


def peer(x, z, c, dz, q, sign):
    dx, dc = q // 2, q % 2
    px = lax.rem(x + sign * dx + 4, 4)
    pz = lax.rem(z + sign * dz + 8, 8)
    pc = lax.rem(c + dc, 2)
    return px * 16 + pz * 2 + pc


def kernel(
    arr_h, tgt_h, slot_h, bank_h, mem_h, csum_h, best_o, cent_o,
    tgt, slot, mem, arr, bank, rn, colc, kbuf, send, recv, scode, zcode, rcode, bests, ret, r8,
    acc, csum, passed, onward, partial, ag,
    in_sem, bank_sem, self_sem, row_ss, row_rs, code_ss, code_rs, ret_ss, ret_rs,
    rs_ss, rs_rs, ag_ss, ag_rs, met, out_sem,
):
    g = lax.axis_index("grp")
    me = lax.axis_index("own")
    x, z, c = me // 16, lax.rem(me // 2, 8), lax.rem(me, 2)
    clusters = mem_h.shape[0]
    quarter = clusters // 4

    barrier = pltpu.get_barrier_semaphore()
    for dz in LINE:
        pl.semaphore_signal(
            barrier, inc=1, device_id=(g, peer(x, z, c, dz, 0, 1)), device_id_type=MESH
        )
    @pl.loop(1, 8)
    def _(q):
        pl.semaphore_signal(
            barrier, inc=1, device_id=(g, peer(x, z, c, 0, q, 1)), device_id_type=MESH
        )
    for j in range(1, 4):
        pl.semaphore_signal(
            barrier, inc=1, device_id=(lax.rem(g + j, 4), me), device_id_type=MESH
        )

    tgt_cp = pltpu.make_async_copy(tgt_h, tgt, in_sem.at[2])
    tgt_cp.start()
    slot_cp = pltpu.make_async_copy(slot_h, slot, in_sem.at[3])
    slot_cp.start()
    arr_cp = pltpu.make_async_copy(arr_h, arr, in_sem.at[0])
    arr_cp.start()
    csum_cp = pltpu.make_async_copy(
        csum_h.at[pl.ds(g * quarter, quarter), :], csum, in_sem.at[1]
    )
    csum_cp.start()
    bank_cp = pltpu.make_async_copy(bank_h, bank, bank_sem)
    bank_cp.start()
    mem_cp = pltpu.make_async_copy(mem_h, mem, in_sem.at[4])
    mem_cp.start()

    tgt_cp.wait()
    t = tgt[...]
    dx = ((t >> 4) - x) & 3
    dz = ((t >> 1) - z) & 7
    dc = (t - c) & 1
    zi_of = jnp.zeros_like(t)
    for zi, d in enumerate(Z_ORDER):
        zi_of = jnp.where(dz == d, zi, zi_of)
    pos = zi_of * 8 + dx * 2 + dc
    rows = t.shape[1]
    hit = lax.broadcasted_iota(jnp.int32, (64, rows), 0) == pos
    upper = (
        lax.broadcasted_iota(jnp.int32, (rows, rows), 0)
        < lax.broadcasted_iota(jnp.int32, (rows, rows), 1)
    ).astype(F32).astype(BF16)
    earlier = jnp.dot(hit.astype(F32).astype(BF16), upper, preferred_element_type=F32)
    placed = jnp.sum(jnp.where(hit, earlier, 0.0), axis=0, keepdims=True).astype(jnp.int32)
    k = pos * 16 + placed
    kbuf[...] = k
    slot_cp.wait()
    code_row = jnp.broadcast_to((slot[...] + 1).astype(F32), (8, rows)).astype(BF16)

    arr_cp.wait()
    values = arr[...].astype(F32)
    unit = (
        values / jnp.sqrt(jnp.sum(values * values, axis=1, keepdims=True) + EPS)
    ).astype(BF16)
    match = (lax.broadcasted_iota(jnp.int32, (1024, rows), 0) == k).astype(F32).astype(BF16)
    send[...] = (
        jnp.dot(match, unit, preferred_element_type=F32).astype(BF16).reshape(64, 16, -1)
    )
    sent_codes = nt(code_row, match)[0:1, :] - 1.0
    for zi in range(8):
        scode[zi] = sent_codes[:, zi * 128 : zi * 128 + 128]

    pl.semaphore_wait(barrier, 17)
    @pl.loop(1, 8)
    def _(q):
        pl.semaphore_signal(
            met, inc=1, device_id=(g, peer(x, z, c, 0, q, 1)), device_id_type=MESH
        )

    def row_copy(zi, lo, n, dev):
        part = pl.ds(zi * 8 + lo, n)
        return pltpu.make_async_remote_copy(
            src_ref=send.at[part], dst_ref=recv.at[part], send_sem=row_ss.at[zi],
            recv_sem=row_rs.at[zi], device_id=(g, dev), device_id_type=MESH,
        )

    def code_z(zi):
        return pltpu.make_async_remote_copy(
            src_ref=scode.at[zi], dst_ref=zcode.at[zi], send_sem=code_ss.at[zi],
            recv_sem=code_rs.at[zi], device_id=(g, peer(x, z, c, Z_ORDER[zi], 0, 1)),
            device_id_type=MESH,
        )

    def code_x(q, dev):
        return pltpu.make_async_remote_copy(
            src_ref=zcode, dst_ref=rcode.at[q], send_sem=code_ss.at[SELF_GROUP],
            recv_sem=code_rs.at[SELF_GROUP], device_id=(g, dev), device_id_type=MESH,
        )

    def codes_x():
        return pltpu.make_async_remote_copy(
            src_ref=rcode.at[pl.ds(1, 7)], dst_ref=rcode.at[pl.ds(1, 7)],
            send_sem=code_ss.at[SELF_GROUP], recv_sem=code_rs.at[SELF_GROUP],
            device_id=(g, me), device_id_type=MESH,
        )

    def ret_copy(zi, q, dev):
        return pltpu.make_async_remote_copy(
            src_ref=bests.at[zi], dst_ref=ret.at[zi * 8 + q], send_sem=ret_ss.at[zi],
            recv_sem=ret_rs.at[zi], device_id=(g, dev), device_id_type=MESH,
        )

    def landed(buf, zi, sem):
        lo = 1 if zi == SELF_GROUP else 0
        part = pl.ds(zi * 8 + lo, 8 - lo)
        return pltpu.make_async_remote_copy(
            src_ref=buf.at[part], dst_ref=buf.at[part], send_sem=sem.at[zi],
            recv_sem=sem.at[zi], device_id=(g, me), device_id_type=MESH,
        )

    def piece(far, half):
        start = lax.rem(g + far, 4) * quarter + half * (quarter // 2)
        return pl.ds(pl.multiple_of(start, quarter // 2), quarter // 2)

    def to_next(src, dst, ss, rs, step, side):
        return pltpu.make_async_remote_copy(
            src_ref=src, dst_ref=dst, send_sem=ss.at[step * 2 + side],
            recv_sem=rs.at[step * 2 + side],
            device_id=(lax.rem(g + (1 if side == 0 else 3), 4), me), device_id_type=MESH,
        )

    me_slot = SELF_GROUP * 8
    self_cp = pltpu.make_async_copy(send.at[me_slot], recv.at[me_slot], self_sem)
    self_cp.start()
    zcode[SELF_GROUP] = scode[SELF_GROUP]

    def send_rows(zi, q):
        dev = peer(x, z, c, Z_ORDER[zi], q, 1)
        row_copy(zi, q, 1, dev).start()

    for dz in LINE:
        code_z(Z_ORDER.index(dz)).start()
        send_rows(Z_ORDER.index(dz), 0)

    @pl.loop(1, 8)
    def _(q):
        send_rows(SELF_GROUP, q)

    pl.semaphore_wait(met, 7)

    for pair in ((4,), (3, 5), (2, 6), (1, 7)):
        @pl.loop(1, 8)
        def _(q):
            for dz in pair:
                send_rows(Z_ORDER.index(dz), q)

    mem_cp.wait()
    @pl.loop(0, clusters)
    def _(cl):
        live = lax.broadcasted_iota(jnp.int32, (32, 128), 0) < mem[cl]
        colc[pl.ds(pl.multiple_of(cl * 32, 32), 32), :] = jnp.where(
            live, jnp.full((32, 128), cl, jnp.int32), -2
        ).astype(F32)

    bank_cp.wait()

    @pl.loop(0, bank.shape[0] // 256)
    def _(i):
        part = pl.ds(pl.multiple_of(i * 256, 256), 256)
        b = bank[part, :].astype(F32)
        norm = 1.0 / jnp.sqrt(jnp.sum(b * b, axis=1, keepdims=True) + EPS)
        rn[part, :] = jnp.broadcast_to(norm, (256, 128))

    for dz in LINE:
        code_z(Z_ORDER.index(dz)).wait_recv()
    rcode[0] = zcode[...]

    @pl.loop(1, 8)
    def _(q):
        code_x(q, peer(x, z, c, 0, q, 1)).start()

    lane16 = lax.broadcasted_iota(jnp.int32, (1, 128), 1) // 16

    def folded(parts):
        total = jnp.zeros((1, 128), F32)
        for q in range(8):
            total = jnp.where(lane16 == q, parts[q], total)
        return total

    def self_lo(zi):
        return 1 if zi == SELF_GROUP else 0

    def keep(chunk, best):
        for h in range(2):
            zi = 2 * chunk + h
            bests[zi] = jnp.max(best[h], axis=0, keepdims=True)
            if zi == SELF_GROUP:
                ret[me_slot] = bests[zi]

    deferred, held = [], None
    acc[...] = jnp.zeros_like(acc)
    for chunk in range(4):
        for zi in (2 * chunk, 2 * chunk + 1):
            lo = self_lo(zi)
            landed(recv, zi, row_rs).wait_recv()
            if lo:
                self_cp.wait()
        if chunk == 0:
            codes_x().wait_recv()
        codes = [
            folded([rcode[q, zi] for q in range(8)]) for zi in (2 * chunk, 2 * chunk + 1)
        ]
        q_rows = recv[pl.ds(chunk * 16, 16)].reshape(256, -1)
        row_of = jnp.concatenate(codes, axis=1)
        which = (
            lax.broadcasted_iota(jnp.int32, (clusters, 256), 0).astype(F32) == row_of
        ).astype(F32).astype(BF16)
        acc[...] += jnp.dot(which, q_rows, preferred_element_type=F32)
        if chunk == 3:
            for side in range(2):
                to_next(acc.at[piece(2, side)], passed.at[side], rs_ss, rs_rs, 0, side).start()

        def tile(i, best, q_rows=q_rows, codes=codes, size=TILE):
            part = pl.ds(pl.multiple_of(i * size, size), size)
            s = nt(bank[part, :], q_rows)
            scale, cols = rn[part, :], colc[part, :]
            new = []
            for h in range(2):
                cand = jnp.where(
                    cols == codes[h], s[:, h * 128 : h * 128 + 128] * scale, -3.0
                ).reshape(size // 8, 8, 128)
                new.append(jnp.maximum(best[h], jnp.max(cand, axis=0)))
            return tuple(new)

        start = jnp.full((8, 128), -3.0, F32)
        tiles = bank.shape[0] // TILE
        if chunk < 2:
            best = lax.fori_loop(
                0, tiles // FACTOR, functools.partial(tile, size=FACTOR * TILE), (start, start)
            )
        elif chunk == 2:
            best = lax.fori_loop(0, tiles - DEFER, tile, (start, start))
            for n in range(DEFER):
                deferred.append(functools.partial(tile, tiles - DEFER + n))
            held = best
        else:
            for step in deferred:
                held = step(held)
            keep(2, held)
            best = (start, start)
            if not deferred:
                best = tile(0, best)
            for side in range(2):
                to_next(
                    acc.at[piece(1 if side == 0 else 3, 1 - side)], partial.at[side, 1 - side],
                    rs_ss, rs_rs, 1, side,
                ).start()
            done = tiles - 1 - DEFER
            best = lax.fori_loop(0 if deferred else 1, done, tile, best)
            for side in range(2):
                to_next(passed.at[side], passed.at[side], rs_ss, rs_rs, 0, side).wait_recv()
                onward[side] = passed[side] + acc[piece(1 if side == 0 else 3, side)]
                to_next(onward.at[side], partial.at[side, side], rs_ss, rs_rs, 2, side).start()
            best = lax.fori_loop(done, tiles, tile, best)
        if chunk != 2:
            keep(chunk, best)

    for zi in range(8):
        @pl.loop(self_lo(zi), 8)
        def _(q):
            ret_copy(zi, q, peer(x, z, c, Z_ORDER[zi], q, -1)).start()

    csum_cp.wait()
    mine = pl.ds(pl.multiple_of(g * quarter, quarter), quarter)
    total = csum[...] + acc[mine, :]
    for side in range(2):
        for step, half in ((1, 1 - side), (2, side)):
            landing = partial.at[side, half]
            to_next(landing, landing, rs_ss, rs_rs, step, side).wait_recv()
        total += partial[side].reshape(quarter, -1)
    unit_total = total / jnp.sqrt(jnp.sum(total * total, axis=1, keepdims=True) + EPS)
    ag[g] = unit_total.reshape(2, quarter // 2, -1)

    def publish(far, half):
        at = lax.rem(g + far, 4)
        return pltpu.make_async_copy(
            ag.at[at, half], cent_o.at[at, half], out_sem.at[far * 2 + half]
        )

    def spread_mine(step):
        for side in range(2):
            half = ag.at[g, side if step == 0 else 1 - side]
            to_next(half, half, ag_ss, ag_rs, step, side).start()
            if step == 0:
                publish(0, side).start()

    spread_mine(0)

    for side in range(2):
        half = ag.at[g, side]
        to_next(half, half, ag_ss, ag_rs, 0, side).wait_send()
    spread_mine(1)
    for side in range(2):
        half = ag.at[lax.rem(g + 3 + 2 * side, 4), side]
        to_next(half, half, ag_ss, ag_rs, 0, side).wait_recv()
        to_next(half, half, ag_ss, ag_rs, 2, side).start()
        publish(3 if side == 0 else 1, side).start()

    for zi in range(8):
        landed(ret, zi, ret_rs).wait_recv()
    for zi in range(8):
        r8[zi : zi + 1, :] = folded([ret[zi * 8 + q] for q in range(8)])
    k = kbuf[...]
    group = (lax.broadcasted_iota(jnp.int32, (8, rows), 0) == (k >> 7)).astype(F32)
    lane_of = lax.broadcasted_iota(jnp.int32, (128, rows), 0)
    spread = lax.dot_general(
        r8[...], group, (((0,), (0,)), ((), ())),
        preferred_element_type=F32, precision=lax.Precision.HIGHEST,
    )
    best_o[...] = jnp.sum(
        jnp.where(lane_of == (k & 127), spread, 0.0), axis=0, keepdims=True
    )

    for side in range(2):
        for step, far, half in ((1, 3 - 2 * side, 1 - side), (2, 2, side)):
            landing = ag.at[lax.rem(g + far, 4), half]
            to_next(landing, landing, ag_ss, ag_rs, step, side).wait_recv()
            publish(far, half).start()
    for far in range(4):
        for half in range(2):
            publish(far, half).wait()

    for zi in range(8):
        landed(send, zi, row_ss).wait_send()
        landed(ret, zi, ret_ss).wait_send()
    for dz in LINE:
        code_z(Z_ORDER.index(dz)).wait_send()
    codes_x().wait_send()
    for step in range(3):
        for side in range(2):
            half = passed.at[side]
            to_next(half, half, rs_ss, rs_rs, step, side).wait_send()
            if step > 0:
                to_next(half, half, ag_ss, ag_rs, step, side).wait_send()


def hand_on(best_i, cent_i, best_o, cent_o, sem):
    copies = [
        pltpu.make_async_copy(best_i, best_o, sem.at[0]),
        pltpu.make_async_copy(cent_i, cent_o, sem.at[1]),
    ]
    for copy in copies:
        copy.start()
    for copy in copies:
        copy.wait()


def body(arrivals, home_owner, cluster_slot, bank, members, centroid_sum):
    rows, width = arrivals.shape
    clusters, depth, _ = bank.shape
    dma = pltpu.SemaphoreType.DMA
    hbm = pl.BlockSpec(memory_space=pl.ANY)
    vmem = pl.BlockSpec(memory_space=pltpu.VMEM)
    best, cent = pl.pallas_call(
        kernel,
        out_shape=(
            jax.ShapeDtypeStruct((1, rows), F32),
            jax.ShapeDtypeStruct((4, 2, clusters // 8, width), F32),
        ),
        in_specs=[hbm] * 6,
        out_specs=(vmem, hbm),
        scratch_shapes=[
            pltpu.VMEM((1, rows), jnp.int32),
            pltpu.VMEM((1, rows), jnp.int32),
            pltpu.SMEM((clusters,), jnp.int32),
            pltpu.VMEM((rows, width), BF16),
            pltpu.VMEM((clusters * depth, width), BF16),
            pltpu.VMEM((clusters * depth, 128), F32),
            pltpu.VMEM((clusters * depth, 128), F32),
            pltpu.VMEM((1, rows), jnp.int32),
            pltpu.VMEM((64, 16, width), BF16),
            pltpu.VMEM((64, 16, width), BF16),
            pltpu.VMEM((8, 1, 128), F32),
            pltpu.VMEM((8, 1, 128), F32),
            pltpu.VMEM((8, 8, 1, 128), F32),
            pltpu.VMEM((8, 1, 128), F32),
            pltpu.VMEM((64, 1, 128), F32),
            pltpu.VMEM((8, 128), F32),
            pltpu.VMEM((clusters, width), F32),
            pltpu.VMEM((clusters // 4, width), F32),
            pltpu.VMEM((2, clusters // 8, width), F32),
            pltpu.VMEM((2, clusters // 8, width), F32),
            pltpu.VMEM((2, 2, clusters // 8, width), F32),
            pltpu.VMEM((4, 2, clusters // 8, width), F32),
            dma((5,)), dma, dma,
            dma((8,)), dma((8,)), dma((8,)), dma((8,)), dma((8,)), dma((8,)),
            dma((6,)), dma((6,)), dma((6,)), dma((6,)),
            pltpu.SemaphoreType.REGULAR, dma((8,)),
        ],
        compiler_params=pltpu.CompilerParams(
            collective_id=0, has_side_effects=True, vmem_limit_bytes=28 << 20
        ),
        name="semdedup_round",
    )(*[
        pltpu.with_memory_space_constraint(a, pltpu.HBM) for a in (
        arrivals,
        home_owner.reshape(1, rows),
        cluster_slot.reshape(1, rows),
        bank.reshape(clusters * depth, width),
        members,
        centroid_sum,
    )])
    best, cent = pl.pallas_call(
        hand_on,
        out_shape=(
            jax.ShapeDtypeStruct(best.shape, F32), jax.ShapeDtypeStruct(cent.shape, F32)
        ),
        in_specs=[hbm, hbm],
        out_specs=(hbm, hbm),
        scratch_shapes=[dma((2,))],
        compiler_params=pltpu.CompilerParams(vmem_limit_bytes=4 << 20),
        name="hand_on",
    )(best, cent)
    return best.reshape(rows), cent.reshape(clusters, width)


def solution(mesh):
    return jax.shard_map(
        body,
        mesh=mesh,
        in_specs=(
            P(("grp", "own"), None),
            P(("grp", "own"), None),
            P(("grp", "own")),
            P("own", None, None),
            P("own"),
            P("own", None),
        ),
        out_specs=(P(("grp", "own")), P("own", None)),
        check_vma=False,
    )
```

```python
import functools

import jax
import jax.numpy as jnp
from jax import lax
from jax.experimental import pallas as pl
from jax.experimental.pallas import tpu as pltpu
from jax.sharding import PartitionSpec as P

EPS = 1e-06
MESH = pl.DeviceIdType.MESH
Z_ORDER = (4, 0, 3, 5, 2, 6, 1, 7)
LINE = (4, 3, 5, 2, 6, 1, 7)
SELF_GROUP = Z_ORDER.index(0)
F32, BF16 = jnp.float32, jnp.bfloat16
TILE = 2048
FACTOR, DEFER = 1, 1


def nt(a, b):
    return lax.dot_general(a, b, (((1,), (1,)), ((), ())), preferred_element_type=F32)


def peer(x, z, c, dz, q, sign):
    dx, dc = q // 2, q % 2
    px = lax.rem(x + sign * dx + 4, 4)
    pz = lax.rem(z + sign * dz + 8, 8)
    pc = lax.rem(c + dc, 2)
    return px * 16 + pz * 2 + pc


def kernel(
    arr_h, tgt_h, slot_h, bank_h, mem_h, csum_h, best_o, cent_o,
    tgt, slot, mem, arr, bank, rn, colc, kbuf, send, recv, scode, zcode, rcode, bests, ret, r8,
    acc, csum, passed, onward, partial, ag,
    in_sem, bank_sem, self_sem, row_ss, row_rs, code_ss, code_rs, ret_ss, ret_rs,
    rs_ss, rs_rs, ag_ss, ag_rs, met,
):
    g = lax.axis_index("grp")
    me = lax.axis_index("own")
    x, z, c = me // 16, lax.rem(me // 2, 8), lax.rem(me, 2)
    clusters = mem_h.shape[0]
    quarter = clusters // 4

    barrier = pltpu.get_barrier_semaphore()
    for dz in LINE:
        pl.semaphore_signal(
            barrier, inc=1, device_id=(g, peer(x, z, c, dz, 0, 1)), device_id_type=MESH
        )
    @pl.loop(1, 8)
    def _(q):
        pl.semaphore_signal(
            barrier, inc=1, device_id=(g, peer(x, z, c, 0, q, 1)), device_id_type=MESH
        )
    for j in range(1, 4):
        pl.semaphore_signal(
            barrier, inc=1, device_id=(lax.rem(g + j, 4), me), device_id_type=MESH
        )

    tgt_cp = pltpu.make_async_copy(tgt_h, tgt, in_sem.at[2])
    tgt_cp.start()
    slot_cp = pltpu.make_async_copy(slot_h, slot, in_sem.at[3])
    slot_cp.start()
    arr_cp = pltpu.make_async_copy(arr_h, arr, in_sem.at[0])
    arr_cp.start()
    csum_cp = pltpu.make_async_copy(
        csum_h.at[pl.ds(g * quarter, quarter), :], csum, in_sem.at[1]
    )
    csum_cp.start()
    bank_cp = pltpu.make_async_copy(bank_h, bank, bank_sem)
    bank_cp.start()
    mem_cp = pltpu.make_async_copy(mem_h, mem, in_sem.at[4])
    mem_cp.start()

    tgt_cp.wait()
    t = tgt[...]
    dx = ((t >> 4) - x) & 3
    dz = ((t >> 1) - z) & 7
    dc = (t - c) & 1
    zi_of = jnp.zeros_like(t)
    for zi, d in enumerate(Z_ORDER):
        zi_of = jnp.where(dz == d, zi, zi_of)
    pos = zi_of * 8 + dx * 2 + dc
    rows = t.shape[1]
    hit = lax.broadcasted_iota(jnp.int32, (64, rows), 0) == pos
    upper = (
        lax.broadcasted_iota(jnp.int32, (rows, rows), 0)
        < lax.broadcasted_iota(jnp.int32, (rows, rows), 1)
    ).astype(F32).astype(BF16)
    earlier = jnp.dot(hit.astype(F32).astype(BF16), upper, preferred_element_type=F32)
    placed = jnp.sum(jnp.where(hit, earlier, 0.0), axis=0, keepdims=True).astype(jnp.int32)
    k = pos * 16 + placed
    kbuf[...] = k
    slot_cp.wait()
    code_row = jnp.broadcast_to((slot[...] + 1).astype(F32), (8, rows)).astype(BF16)

    arr_cp.wait()
    values = arr[...].astype(F32)
    unit = (
        values / jnp.sqrt(jnp.sum(values * values, axis=1, keepdims=True) + EPS)
    ).astype(BF16)
    match = (lax.broadcasted_iota(jnp.int32, (1024, rows), 0) == k).astype(F32).astype(BF16)
    send[...] = (
        jnp.dot(match, unit, preferred_element_type=F32).astype(BF16).reshape(64, 16, -1)
    )
    sent_codes = nt(code_row, match)[0:1, :] - 1.0
    for zi in range(8):
        scode[zi] = sent_codes[:, zi * 128 : zi * 128 + 128]

    pl.semaphore_wait(barrier, 17)
    @pl.loop(1, 8)
    def _(q):
        pl.semaphore_signal(
            met, inc=1, device_id=(g, peer(x, z, c, 0, q, 1)), device_id_type=MESH
        )

    def row_copy(zi, lo, n, dev):
        part = pl.ds(zi * 8 + lo, n)
        return pltpu.make_async_remote_copy(
            src_ref=send.at[part], dst_ref=recv.at[part], send_sem=row_ss.at[zi],
            recv_sem=row_rs.at[zi], device_id=(g, dev), device_id_type=MESH,
        )

    def code_z(zi):
        return pltpu.make_async_remote_copy(
            src_ref=scode.at[zi], dst_ref=zcode.at[zi], send_sem=code_ss.at[zi],
            recv_sem=code_rs.at[zi], device_id=(g, peer(x, z, c, Z_ORDER[zi], 0, 1)),
            device_id_type=MESH,
        )

    def code_x(q, dev):
        return pltpu.make_async_remote_copy(
            src_ref=zcode, dst_ref=rcode.at[q], send_sem=code_ss.at[SELF_GROUP],
            recv_sem=code_rs.at[SELF_GROUP], device_id=(g, dev), device_id_type=MESH,
        )

    def codes_x():
        return pltpu.make_async_remote_copy(
            src_ref=rcode.at[pl.ds(1, 7)], dst_ref=rcode.at[pl.ds(1, 7)],
            send_sem=code_ss.at[SELF_GROUP], recv_sem=code_rs.at[SELF_GROUP],
            device_id=(g, me), device_id_type=MESH,
        )

    def ret_copy(zi, q, dev):
        return pltpu.make_async_remote_copy(
            src_ref=bests.at[zi], dst_ref=ret.at[zi * 8 + q], send_sem=ret_ss.at[zi],
            recv_sem=ret_rs.at[zi], device_id=(g, dev), device_id_type=MESH,
        )

    def landed(buf, zi, sem):
        lo = 1 if zi == SELF_GROUP else 0
        part = pl.ds(zi * 8 + lo, 8 - lo)
        return pltpu.make_async_remote_copy(
            src_ref=buf.at[part], dst_ref=buf.at[part], send_sem=sem.at[zi],
            recv_sem=sem.at[zi], device_id=(g, me), device_id_type=MESH,
        )

    def piece(far, half):
        start = lax.rem(g + far, 4) * quarter + half * (quarter // 2)
        return pl.ds(pl.multiple_of(start, quarter // 2), quarter // 2)

    def to_next(src, dst, ss, rs, step, side):
        return pltpu.make_async_remote_copy(
            src_ref=src, dst_ref=dst, send_sem=ss.at[step * 2 + side],
            recv_sem=rs.at[step * 2 + side],
            device_id=(lax.rem(g + (1 if side == 0 else 3), 4), me), device_id_type=MESH,
        )

    me_slot = SELF_GROUP * 8
    self_cp = pltpu.make_async_copy(send.at[me_slot], recv.at[me_slot], self_sem)
    self_cp.start()
    zcode[SELF_GROUP] = scode[SELF_GROUP]

    def send_rows(zi, q):
        dev = peer(x, z, c, Z_ORDER[zi], q, 1)
        row_copy(zi, q, 1, dev).start()

    for dz in LINE:
        code_z(Z_ORDER.index(dz)).start()
        send_rows(Z_ORDER.index(dz), 0)

    @pl.loop(1, 8)
    def _(q):
        send_rows(SELF_GROUP, q)

    pl.semaphore_wait(met, 7)

    for pair in ((4,), (3, 5), (2, 6), (1, 7)):
        @pl.loop(1, 8)
        def _(q):
            for dz in pair:
                send_rows(Z_ORDER.index(dz), q)

    mem_cp.wait()
    @pl.loop(0, clusters)
    def _(cl):
        live = lax.broadcasted_iota(jnp.int32, (32, 128), 0) < mem[cl]
        colc[pl.ds(pl.multiple_of(cl * 32, 32), 32), :] = jnp.where(
            live, jnp.full((32, 128), cl, jnp.int32), -2
        ).astype(F32)

    bank_cp.wait()

    @pl.loop(0, bank.shape[0] // 256)
    def _(i):
        part = pl.ds(pl.multiple_of(i * 256, 256), 256)
        b = bank[part, :].astype(F32)
        norm = 1.0 / jnp.sqrt(jnp.sum(b * b, axis=1, keepdims=True) + EPS)
        rn[part, :] = jnp.broadcast_to(norm, (256, 128))

    for dz in LINE:
        code_z(Z_ORDER.index(dz)).wait_recv()
    rcode[0] = zcode[...]

    @pl.loop(1, 8)
    def _(q):
        code_x(q, peer(x, z, c, 0, q, 1)).start()

    lane16 = lax.broadcasted_iota(jnp.int32, (1, 128), 1) // 16

    def folded(parts):
        total = jnp.zeros((1, 128), F32)
        for q in range(8):
            total = jnp.where(lane16 == q, parts[q], total)
        return total

    def self_lo(zi):
        return 1 if zi == SELF_GROUP else 0

    def keep(chunk, best):
        for h in range(2):
            zi = 2 * chunk + h
            bests[zi] = jnp.max(best[h], axis=0, keepdims=True)
            if zi == SELF_GROUP:
                ret[me_slot] = bests[zi]

    deferred, held = [], None
    acc[...] = jnp.zeros_like(acc)
    for chunk in range(4):
        for zi in (2 * chunk, 2 * chunk + 1):
            lo = self_lo(zi)
            landed(recv, zi, row_rs).wait_recv()
            if lo:
                self_cp.wait()
        if chunk == 0:
            codes_x().wait_recv()
        codes = [
            folded([rcode[q, zi] for q in range(8)]) for zi in (2 * chunk, 2 * chunk + 1)
        ]
        q_rows = recv[pl.ds(chunk * 16, 16)].reshape(256, -1)
        row_of = jnp.concatenate(codes, axis=1)
        which = (
            lax.broadcasted_iota(jnp.int32, (clusters, 256), 0).astype(F32) == row_of
        ).astype(F32).astype(BF16)
        acc[...] += jnp.dot(which, q_rows, preferred_element_type=F32)
        if chunk == 3:
            for side in range(2):
                to_next(acc.at[piece(2, side)], passed.at[side], rs_ss, rs_rs, 0, side).start()

        def tile(i, best, q_rows=q_rows, codes=codes, size=TILE):
            part = pl.ds(pl.multiple_of(i * size, size), size)
            s = nt(bank[part, :], q_rows)
            scale, cols = rn[part, :], colc[part, :]
            new = []
            for h in range(2):
                cand = jnp.where(
                    cols == codes[h], s[:, h * 128 : h * 128 + 128] * scale, -3.0
                ).reshape(size // 8, 8, 128)
                new.append(jnp.maximum(best[h], jnp.max(cand, axis=0)))
            return tuple(new)

        start = jnp.full((8, 128), -3.0, F32)
        tiles = bank.shape[0] // TILE
        if chunk < 2:
            best = lax.fori_loop(
                0, tiles // FACTOR, functools.partial(tile, size=FACTOR * TILE), (start, start)
            )
        elif chunk == 2:
            best = lax.fori_loop(0, tiles - DEFER, tile, (start, start))
            for n in range(DEFER):
                deferred.append(functools.partial(tile, tiles - DEFER + n))
            held = best
        else:
            for step in deferred:
                held = step(held)
            keep(2, held)
            best = (start, start)
            if not deferred:
                best = tile(0, best)
            for side in range(2):
                to_next(
                    acc.at[piece(1 if side == 0 else 3, 1 - side)], partial.at[side, 1 - side],
                    rs_ss, rs_rs, 1, side,
                ).start()
            done = tiles - 1 - DEFER
            best = lax.fori_loop(0 if deferred else 1, done, tile, best)
            for side in range(2):
                to_next(passed.at[side], passed.at[side], rs_ss, rs_rs, 0, side).wait_recv()
                onward[side] = passed[side] + acc[piece(1 if side == 0 else 3, side)]
                to_next(onward.at[side], partial.at[side, side], rs_ss, rs_rs, 2, side).start()
            best = lax.fori_loop(done, tiles, tile, best)
        if chunk != 2:
            keep(chunk, best)

    for zi in range(8):
        @pl.loop(self_lo(zi), 8)
        def _(q):
            ret_copy(zi, q, peer(x, z, c, Z_ORDER[zi], q, -1)).start()

    csum_cp.wait()
    mine = pl.ds(pl.multiple_of(g * quarter, quarter), quarter)
    total = csum[...] + acc[mine, :]
    for side in range(2):
        for step, half in ((1, 1 - side), (2, side)):
            landing = partial.at[side, half]
            to_next(landing, landing, rs_ss, rs_rs, step, side).wait_recv()
        total += partial[side].reshape(quarter, -1)
    unit_total = total / jnp.sqrt(jnp.sum(total * total, axis=1, keepdims=True) + EPS)
    ag[g] = unit_total.reshape(2, quarter // 2, -1)

    def publish(far, half):
        at = lax.rem(g + far, 4)
        cent_o[at, half] = ag[at, half]

    def spread_mine(step):
        for side in range(2):
            half = ag.at[g, side if step == 0 else 1 - side]
            to_next(half, half, ag_ss, ag_rs, step, side).start()
            if step == 0:
                publish(0, side)

    spread_mine(0)

    for side in range(2):
        half = ag.at[g, side]
        to_next(half, half, ag_ss, ag_rs, 0, side).wait_send()
    spread_mine(1)
    for side in range(2):
        half = ag.at[lax.rem(g + 3 + 2 * side, 4), side]
        to_next(half, half, ag_ss, ag_rs, 0, side).wait_recv()
        to_next(half, half, ag_ss, ag_rs, 2, side).start()
        publish(3 if side == 0 else 1, side)

    for zi in range(8):
        landed(ret, zi, ret_rs).wait_recv()
    for zi in range(8):
        r8[zi : zi + 1, :] = folded([ret[zi * 8 + q] for q in range(8)])
    k = kbuf[...]
    group = (lax.broadcasted_iota(jnp.int32, (8, rows), 0) == (k >> 7)).astype(F32)
    lane_of = lax.broadcasted_iota(jnp.int32, (128, rows), 0)
    spread = lax.dot_general(
        r8[...], group, (((0,), (0,)), ((), ())),
        preferred_element_type=F32, precision=lax.Precision.HIGHEST,
    )
    best_o[...] = jnp.sum(
        jnp.where(lane_of == (k & 127), spread, 0.0), axis=0, keepdims=True
    )

    for side in range(2):
        for step, far, half in ((1, 3 - 2 * side, 1 - side), (2, 2, side)):
            landing = ag.at[lax.rem(g + far, 4), half]
            to_next(landing, landing, ag_ss, ag_rs, step, side).wait_recv()
            publish(far, half)

    for zi in range(8):
        landed(send, zi, row_ss).wait_send()
        landed(ret, zi, ret_ss).wait_send()
    for dz in LINE:
        code_z(Z_ORDER.index(dz)).wait_send()
    codes_x().wait_send()
    for step in range(3):
        for side in range(2):
            half = passed.at[side]
            to_next(half, half, rs_ss, rs_rs, step, side).wait_send()
            if step > 0:
                to_next(half, half, ag_ss, ag_rs, step, side).wait_send()


def hand_on(best_i, cent_i, best_o, cent_o, sem):
    copies = [
        pltpu.make_async_copy(best_i, best_o, sem.at[0]),
        pltpu.make_async_copy(cent_i, cent_o, sem.at[1]),
    ]
    for copy in copies:
        copy.start()
    for copy in copies:
        copy.wait()


def body(arrivals, home_owner, cluster_slot, bank, members, centroid_sum):
    rows, width = arrivals.shape
    clusters, depth, _ = bank.shape
    dma = pltpu.SemaphoreType.DMA
    hbm = pl.BlockSpec(memory_space=pl.ANY)
    vmem = pl.BlockSpec(memory_space=pltpu.VMEM)
    best, cent = pl.pallas_call(
        kernel,
        out_shape=(
            jax.ShapeDtypeStruct((1, rows), F32),
            jax.ShapeDtypeStruct((4, 2, clusters // 8, width), F32),
        ),
        in_specs=[hbm] * 6,
        out_specs=(vmem, vmem),
        scratch_shapes=[
            pltpu.VMEM((1, rows), jnp.int32),
            pltpu.VMEM((1, rows), jnp.int32),
            pltpu.SMEM((clusters,), jnp.int32),
            pltpu.VMEM((rows, width), BF16),
            pltpu.VMEM((clusters * depth, width), BF16),
            pltpu.VMEM((clusters * depth, 128), F32),
            pltpu.VMEM((clusters * depth, 128), F32),
            pltpu.VMEM((1, rows), jnp.int32),
            pltpu.VMEM((64, 16, width), BF16),
            pltpu.VMEM((64, 16, width), BF16),
            pltpu.VMEM((8, 1, 128), F32),
            pltpu.VMEM((8, 1, 128), F32),
            pltpu.VMEM((8, 8, 1, 128), F32),
            pltpu.VMEM((8, 1, 128), F32),
            pltpu.VMEM((64, 1, 128), F32),
            pltpu.VMEM((8, 128), F32),
            pltpu.VMEM((clusters, width), F32),
            pltpu.VMEM((clusters // 4, width), F32),
            pltpu.VMEM((2, clusters // 8, width), F32),
            pltpu.VMEM((2, clusters // 8, width), F32),
            pltpu.VMEM((2, 2, clusters // 8, width), F32),
            pltpu.VMEM((4, 2, clusters // 8, width), F32),
            dma((5,)), dma, dma,
            dma((8,)), dma((8,)), dma((8,)), dma((8,)), dma((8,)), dma((8,)),
            dma((6,)), dma((6,)), dma((6,)), dma((6,)),
            pltpu.SemaphoreType.REGULAR,
        ],
        compiler_params=pltpu.CompilerParams(
            collective_id=0, has_side_effects=True, vmem_limit_bytes=28 << 20
        ),
        name="semdedup_round",
    )(*[
        pltpu.with_memory_space_constraint(a, pltpu.HBM) for a in (
        arrivals,
        home_owner.reshape(1, rows),
        cluster_slot.reshape(1, rows),
        bank.reshape(clusters * depth, width),
        members,
        centroid_sum,
    )])
    best, cent = pl.pallas_call(
        hand_on,
        out_shape=(
            jax.ShapeDtypeStruct(best.shape, F32), jax.ShapeDtypeStruct(cent.shape, F32)
        ),
        in_specs=[hbm, hbm],
        out_specs=(hbm, hbm),
        scratch_shapes=[dma((2,))],
        compiler_params=pltpu.CompilerParams(vmem_limit_bytes=4 << 20),
        name="hand_on",
    )(best, cent)
    return best.reshape(rows), cent.reshape(clusters, width)


def solution(mesh):
    return jax.shard_map(
        body,
        mesh=mesh,
        in_specs=(
            P(("grp", "own"), None),
            P(("grp", "own"), None),
            P(("grp", "own")),
            P("own", None, None),
            P("own"),
            P("own", None),
        ),
        out_specs=(P(("grp", "own")), P("own", None)),
        check_vma=False,
    )
```

```python
import functools

import jax
import jax.numpy as jnp
from jax import lax
from jax.experimental import pallas as pl
from jax.experimental.pallas import tpu as pltpu
from jax.sharding import PartitionSpec as P

EPS = 1e-06
MESH = pl.DeviceIdType.MESH
Z_ORDER = (4, 0, 3, 5, 2, 6, 1, 7)
LINE = (4, 3, 5, 2, 6, 1, 7)
SELF_GROUP = Z_ORDER.index(0)
F32, BF16 = jnp.float32, jnp.bfloat16
TILE = 2048
FACTOR, DEFER = 2, 2


def nt(a, b):
    return lax.dot_general(a, b, (((1,), (1,)), ((), ())), preferred_element_type=F32)


def peer(x, z, c, dz, q, sign):
    dx, dc = q // 2, q % 2
    px = lax.rem(x + sign * dx + 4, 4)
    pz = lax.rem(z + sign * dz + 8, 8)
    pc = lax.rem(c + dc, 2)
    return px * 16 + pz * 2 + pc


def kernel(
    arr_h, tgt_h, slot_h, bank_h, mem_h, csum_h, best_o, cent_o,
    tgt, slot, mem, arr, bank, rn, colc, kbuf, send, recv, scode, zcode, rcode, bests, ret, r8,
    acc, csum, passed, onward, partial, ag,
    in_sem, bank_sem, self_sem, row_ss, row_rs, code_ss, code_rs, ret_ss, ret_rs,
    rs_ss, rs_rs, ag_ss, ag_rs, met,
):
    g = lax.axis_index("grp")
    me = lax.axis_index("own")
    x, z, c = me // 16, lax.rem(me // 2, 8), lax.rem(me, 2)
    clusters = mem_h.shape[0]
    quarter = clusters // 4

    barrier = pltpu.get_barrier_semaphore()
    for dz in LINE:
        pl.semaphore_signal(
            barrier, inc=1, device_id=(g, peer(x, z, c, dz, 0, 1)), device_id_type=MESH
        )
    @pl.loop(1, 8)
    def _(q):
        pl.semaphore_signal(
            barrier, inc=1, device_id=(g, peer(x, z, c, 0, q, 1)), device_id_type=MESH
        )
    for j in range(1, 4):
        pl.semaphore_signal(
            barrier, inc=1, device_id=(lax.rem(g + j, 4), me), device_id_type=MESH
        )

    tgt_cp = pltpu.make_async_copy(tgt_h, tgt, in_sem.at[2])
    tgt_cp.start()
    slot_cp = pltpu.make_async_copy(slot_h, slot, in_sem.at[3])
    slot_cp.start()
    arr_cp = pltpu.make_async_copy(arr_h, arr, in_sem.at[0])
    arr_cp.start()
    csum_cp = pltpu.make_async_copy(
        csum_h.at[pl.ds(g * quarter, quarter), :], csum, in_sem.at[1]
    )
    csum_cp.start()
    bank_cp = pltpu.make_async_copy(bank_h, bank, bank_sem)
    bank_cp.start()
    mem_cp = pltpu.make_async_copy(mem_h, mem, in_sem.at[4])
    mem_cp.start()

    tgt_cp.wait()
    t = tgt[...]
    dx = ((t >> 4) - x) & 3
    dz = ((t >> 1) - z) & 7
    dc = (t - c) & 1
    zi_of = jnp.zeros_like(t)
    for zi, d in enumerate(Z_ORDER):
        zi_of = jnp.where(dz == d, zi, zi_of)
    pos = zi_of * 8 + dx * 2 + dc
    rows = t.shape[1]
    hit = lax.broadcasted_iota(jnp.int32, (64, rows), 0) == pos
    upper = (
        lax.broadcasted_iota(jnp.int32, (rows, rows), 0)
        < lax.broadcasted_iota(jnp.int32, (rows, rows), 1)
    ).astype(F32).astype(BF16)
    earlier = jnp.dot(hit.astype(F32).astype(BF16), upper, preferred_element_type=F32)
    placed = jnp.sum(jnp.where(hit, earlier, 0.0), axis=0, keepdims=True).astype(jnp.int32)
    k = pos * 16 + placed
    kbuf[...] = k
    slot_cp.wait()
    code_row = jnp.broadcast_to((slot[...] + 1).astype(F32), (8, rows)).astype(BF16)

    arr_cp.wait()
    values = arr[...].astype(F32)
    unit = (
        values / jnp.sqrt(jnp.sum(values * values, axis=1, keepdims=True) + EPS)
    ).astype(BF16)
    match = (lax.broadcasted_iota(jnp.int32, (1024, rows), 0) == k).astype(F32).astype(BF16)
    send[...] = (
        jnp.dot(match, unit, preferred_element_type=F32).astype(BF16).reshape(64, 16, -1)
    )
    sent_codes = nt(code_row, match)[0:1, :] - 1.0
    for zi in range(8):
        scode[zi] = sent_codes[:, zi * 128 : zi * 128 + 128]

    pl.semaphore_wait(barrier, 17)
    @pl.loop(1, 8)
    def _(q):
        pl.semaphore_signal(
            met, inc=1, device_id=(g, peer(x, z, c, 0, q, 1)), device_id_type=MESH
        )

    def row_copy(zi, lo, n, dev):
        part = pl.ds(zi * 8 + lo, n)
        return pltpu.make_async_remote_copy(
            src_ref=send.at[part], dst_ref=recv.at[part], send_sem=row_ss.at[zi],
            recv_sem=row_rs.at[zi], device_id=(g, dev), device_id_type=MESH,
        )

    def code_z(zi):
        return pltpu.make_async_remote_copy(
            src_ref=scode.at[zi], dst_ref=zcode.at[zi], send_sem=code_ss.at[zi],
            recv_sem=code_rs.at[zi], device_id=(g, peer(x, z, c, Z_ORDER[zi], 0, 1)),
            device_id_type=MESH,
        )

    def code_x(q, dev):
        return pltpu.make_async_remote_copy(
            src_ref=zcode, dst_ref=rcode.at[q], send_sem=code_ss.at[SELF_GROUP],
            recv_sem=code_rs.at[SELF_GROUP], device_id=(g, dev), device_id_type=MESH,
        )

    def codes_x():
        return pltpu.make_async_remote_copy(
            src_ref=rcode.at[pl.ds(1, 7)], dst_ref=rcode.at[pl.ds(1, 7)],
            send_sem=code_ss.at[SELF_GROUP], recv_sem=code_rs.at[SELF_GROUP],
            device_id=(g, me), device_id_type=MESH,
        )

    def ret_copy(zi, q, dev):
        return pltpu.make_async_remote_copy(
            src_ref=bests.at[zi], dst_ref=ret.at[zi * 8 + q], send_sem=ret_ss.at[zi],
            recv_sem=ret_rs.at[zi], device_id=(g, dev), device_id_type=MESH,
        )

    def landed(buf, zi, sem):
        lo = 1 if zi == SELF_GROUP else 0
        part = pl.ds(zi * 8 + lo, 8 - lo)
        return pltpu.make_async_remote_copy(
            src_ref=buf.at[part], dst_ref=buf.at[part], send_sem=sem.at[zi],
            recv_sem=sem.at[zi], device_id=(g, me), device_id_type=MESH,
        )

    def piece(far, half):
        start = lax.rem(g + far, 4) * quarter + half * (quarter // 2)
        return pl.ds(pl.multiple_of(start, quarter // 2), quarter // 2)

    def to_next(src, dst, ss, rs, step, side):
        return pltpu.make_async_remote_copy(
            src_ref=src, dst_ref=dst, send_sem=ss.at[step * 2 + side],
            recv_sem=rs.at[step * 2 + side],
            device_id=(lax.rem(g + (1 if side == 0 else 3), 4), me), device_id_type=MESH,
        )

    me_slot = SELF_GROUP * 8
    self_cp = pltpu.make_async_copy(send.at[me_slot], recv.at[me_slot], self_sem)
    self_cp.start()
    zcode[SELF_GROUP] = scode[SELF_GROUP]

    def send_rows(zi, q):
        dev = peer(x, z, c, Z_ORDER[zi], q, 1)
        row_copy(zi, q, 1, dev).start()

    for dz in LINE:
        code_z(Z_ORDER.index(dz)).start()
        send_rows(Z_ORDER.index(dz), 0)

    @pl.loop(1, 8)
    def _(q):
        send_rows(SELF_GROUP, q)

    pl.semaphore_wait(met, 7)

    for pair in ((4,), (3, 5), (2, 6), (1, 7)):
        @pl.loop(1, 8)
        def _(q):
            for dz in pair:
                send_rows(Z_ORDER.index(dz), q)

    mem_cp.wait()
    @pl.loop(0, clusters)
    def _(cl):
        live = lax.broadcasted_iota(jnp.int32, (32, 128), 0) < mem[cl]
        colc[pl.ds(pl.multiple_of(cl * 32, 32), 32), :] = jnp.where(
            live, jnp.full((32, 128), cl, jnp.int32), -2
        ).astype(F32)

    bank_cp.wait()

    @pl.loop(0, bank.shape[0] // 256)
    def _(i):
        part = pl.ds(pl.multiple_of(i * 256, 256), 256)
        b = bank[part, :].astype(F32)
        norm = 1.0 / jnp.sqrt(jnp.sum(b * b, axis=1, keepdims=True) + EPS)
        rn[part, :] = jnp.broadcast_to(norm, (256, 128))

    for dz in LINE:
        code_z(Z_ORDER.index(dz)).wait_recv()
    rcode[0] = zcode[...]

    @pl.loop(1, 8)
    def _(q):
        code_x(q, peer(x, z, c, 0, q, 1)).start()

    lane16 = lax.broadcasted_iota(jnp.int32, (1, 128), 1) // 16

    def folded(parts):
        total = jnp.zeros((1, 128), F32)
        for q in range(8):
            total = jnp.where(lane16 == q, parts[q], total)
        return total

    def self_lo(zi):
        return 1 if zi == SELF_GROUP else 0

    def keep(chunk, best):
        for h in range(2):
            zi = 2 * chunk + h
            bests[zi] = jnp.max(best[h], axis=0, keepdims=True)
            if zi == SELF_GROUP:
                ret[me_slot] = bests[zi]

    deferred, held = [], None
    acc[...] = jnp.zeros_like(acc)
    for chunk in range(4):
        for zi in (2 * chunk, 2 * chunk + 1):
            lo = self_lo(zi)
            landed(recv, zi, row_rs).wait_recv()
            if lo:
                self_cp.wait()
        if chunk == 0:
            codes_x().wait_recv()
        codes = [
            folded([rcode[q, zi] for q in range(8)]) for zi in (2 * chunk, 2 * chunk + 1)
        ]
        q_rows = recv[pl.ds(chunk * 16, 16)].reshape(256, -1)
        row_of = jnp.concatenate(codes, axis=1)
        which = (
            lax.broadcasted_iota(jnp.int32, (clusters, 256), 0).astype(F32) == row_of
        ).astype(F32).astype(BF16)
        acc[...] += jnp.dot(which, q_rows, preferred_element_type=F32)
        if chunk == 3:
            for side in range(2):
                to_next(acc.at[piece(2, side)], passed.at[side], rs_ss, rs_rs, 0, side).start()

        def tile(i, best, q_rows=q_rows, codes=codes, size=TILE):
            part = pl.ds(pl.multiple_of(i * size, size), size)
            s = nt(bank[part, :], q_rows)
            scale, cols = rn[part, :], colc[part, :]
            new = []
            for h in range(2):
                cand = jnp.where(
                    cols == codes[h], s[:, h * 128 : h * 128 + 128] * scale, -3.0
                ).reshape(size // 8, 8, 128)
                new.append(jnp.maximum(best[h], jnp.max(cand, axis=0)))
            return tuple(new)

        start = jnp.full((8, 128), -3.0, F32)
        tiles = bank.shape[0] // TILE
        if chunk < 2:
            best = lax.fori_loop(
                0, tiles // FACTOR, functools.partial(tile, size=FACTOR * TILE), (start, start)
            )
        elif chunk == 2:
            best = lax.fori_loop(0, tiles - DEFER, tile, (start, start))
            for n in range(DEFER):
                deferred.append(functools.partial(tile, tiles - DEFER + n))
            held = best
        else:
            for step in deferred:
                held = step(held)
            keep(2, held)
            best = (start, start)
            if not deferred:
                best = tile(0, best)
            for side in range(2):
                to_next(
                    acc.at[piece(1 if side == 0 else 3, 1 - side)], partial.at[side, 1 - side],
                    rs_ss, rs_rs, 1, side,
                ).start()
            done = tiles - 1 - DEFER
            best = lax.fori_loop(0 if deferred else 1, done, tile, best)
            for side in range(2):
                to_next(passed.at[side], passed.at[side], rs_ss, rs_rs, 0, side).wait_recv()
                onward[side] = passed[side] + acc[piece(1 if side == 0 else 3, side)]
                to_next(onward.at[side], partial.at[side, side], rs_ss, rs_rs, 2, side).start()
            best = lax.fori_loop(done, tiles, tile, best)
        if chunk != 2:
            keep(chunk, best)

    for zi in range(8):
        @pl.loop(self_lo(zi), 8)
        def _(q):
            ret_copy(zi, q, peer(x, z, c, Z_ORDER[zi], q, -1)).start()

    csum_cp.wait()
    mine = pl.ds(pl.multiple_of(g * quarter, quarter), quarter)
    total = csum[...] + acc[mine, :]
    for side in range(2):
        for step, half in ((1, 1 - side), (2, side)):
            landing = partial.at[side, half]
            to_next(landing, landing, rs_ss, rs_rs, step, side).wait_recv()
        total += partial[side].reshape(quarter, -1)
    unit_total = total / jnp.sqrt(jnp.sum(total * total, axis=1, keepdims=True) + EPS)
    ag[g] = unit_total.reshape(2, quarter // 2, -1)

    def publish(far, half):
        at = lax.rem(g + far, 4)
        cent_o[at, half] = ag[at, half]

    def spread_mine(step):
        for side in range(2):
            half = ag.at[g, side if step == 0 else 1 - side]
            to_next(half, half, ag_ss, ag_rs, step, side).start()
            if step == 0:
                publish(0, side)

    spread_mine(0)

    for side in range(2):
        half = ag.at[g, side]
        to_next(half, half, ag_ss, ag_rs, 0, side).wait_send()
    spread_mine(1)
    for side in range(2):
        half = ag.at[lax.rem(g + 3 + 2 * side, 4), side]
        to_next(half, half, ag_ss, ag_rs, 0, side).wait_recv()
        to_next(half, half, ag_ss, ag_rs, 2, side).start()
        publish(3 if side == 0 else 1, side)

    for zi in range(8):
        landed(ret, zi, ret_rs).wait_recv()
    for zi in range(8):
        r8[zi : zi + 1, :] = folded([ret[zi * 8 + q] for q in range(8)])
    k = kbuf[...]
    group = (lax.broadcasted_iota(jnp.int32, (8, rows), 0) == (k >> 7)).astype(F32)
    lane_of = lax.broadcasted_iota(jnp.int32, (128, rows), 0)
    spread = lax.dot_general(
        r8[...], group, (((0,), (0,)), ((), ())),
        preferred_element_type=F32, precision=lax.Precision.HIGHEST,
    )
    best_o[...] = jnp.sum(
        jnp.where(lane_of == (k & 127), spread, 0.0), axis=0, keepdims=True
    )

    for side in range(2):
        for step, far, half in ((1, 3 - 2 * side, 1 - side), (2, 2, side)):
            landing = ag.at[lax.rem(g + far, 4), half]
            to_next(landing, landing, ag_ss, ag_rs, step, side).wait_recv()
            publish(far, half)

    for zi in range(8):
        landed(send, zi, row_ss).wait_send()
        landed(ret, zi, ret_ss).wait_send()
    for dz in LINE:
        code_z(Z_ORDER.index(dz)).wait_send()
    codes_x().wait_send()
    for step in range(3):
        for side in range(2):
            half = passed.at[side]
            to_next(half, half, rs_ss, rs_rs, step, side).wait_send()
            if step > 0:
                to_next(half, half, ag_ss, ag_rs, step, side).wait_send()


def hand_on(best_i, cent_i, best_o, cent_o, sem):
    copies = [
        pltpu.make_async_copy(best_i, best_o, sem.at[0]),
        pltpu.make_async_copy(cent_i, cent_o, sem.at[1]),
    ]
    for copy in copies:
        copy.start()
    for copy in copies:
        copy.wait()


def body(arrivals, home_owner, cluster_slot, bank, members, centroid_sum):
    rows, width = arrivals.shape
    clusters, depth, _ = bank.shape
    dma = pltpu.SemaphoreType.DMA
    hbm = pl.BlockSpec(memory_space=pl.ANY)
    vmem = pl.BlockSpec(memory_space=pltpu.VMEM)
    best, cent = pl.pallas_call(
        kernel,
        out_shape=(
            jax.ShapeDtypeStruct((1, rows), F32),
            jax.ShapeDtypeStruct((4, 2, clusters // 8, width), F32),
        ),
        in_specs=[hbm] * 6,
        out_specs=(vmem, vmem),
        scratch_shapes=[
            pltpu.VMEM((1, rows), jnp.int32),
            pltpu.VMEM((1, rows), jnp.int32),
            pltpu.SMEM((clusters,), jnp.int32),
            pltpu.VMEM((rows, width), BF16),
            pltpu.VMEM((clusters * depth, width), BF16),
            pltpu.VMEM((clusters * depth, 128), F32),
            pltpu.VMEM((clusters * depth, 128), F32),
            pltpu.VMEM((1, rows), jnp.int32),
            pltpu.VMEM((64, 16, width), BF16),
            pltpu.VMEM((64, 16, width), BF16),
            pltpu.VMEM((8, 1, 128), F32),
            pltpu.VMEM((8, 1, 128), F32),
            pltpu.VMEM((8, 8, 1, 128), F32),
            pltpu.VMEM((8, 1, 128), F32),
            pltpu.VMEM((64, 1, 128), F32),
            pltpu.VMEM((8, 128), F32),
            pltpu.VMEM((clusters, width), F32),
            pltpu.VMEM((clusters // 4, width), F32),
            pltpu.VMEM((2, clusters // 8, width), F32),
            pltpu.VMEM((2, clusters // 8, width), F32),
            pltpu.VMEM((2, 2, clusters // 8, width), F32),
            pltpu.VMEM((4, 2, clusters // 8, width), F32),
            dma((5,)), dma, dma,
            dma((8,)), dma((8,)), dma((8,)), dma((8,)), dma((8,)), dma((8,)),
            dma((6,)), dma((6,)), dma((6,)), dma((6,)),
            pltpu.SemaphoreType.REGULAR,
        ],
        compiler_params=pltpu.CompilerParams(
            collective_id=0, has_side_effects=True, vmem_limit_bytes=28 << 20
        ),
        name="semdedup_round",
    )(*[
        pltpu.with_memory_space_constraint(a, pltpu.HBM) for a in (
        arrivals,
        home_owner.reshape(1, rows),
        cluster_slot.reshape(1, rows),
        bank.reshape(clusters * depth, width),
        members,
        centroid_sum,
    )])
    best, cent = pl.pallas_call(
        hand_on,
        out_shape=(
            jax.ShapeDtypeStruct(best.shape, F32), jax.ShapeDtypeStruct(cent.shape, F32)
        ),
        in_specs=[hbm, hbm],
        out_specs=(hbm, hbm),
        scratch_shapes=[dma((2,))],
        compiler_params=pltpu.CompilerParams(vmem_limit_bytes=4 << 20),
        name="hand_on",
    )(best, cent)
    return best.reshape(rows), cent.reshape(clusters, width)


def solution(mesh):
    return jax.shard_map(
        body,
        mesh=mesh,
        in_specs=(
            P(("grp", "own"), None),
            P(("grp", "own"), None),
            P(("grp", "own")),
            P("own", None, None),
            P("own"),
            P("own", None),
        ),
        out_specs=(P(("grp", "own")), P("own", None)),
        check_vma=False,
    )
```
